256 devices in a mesh: rows: 64 (over z, x, core), coil: 4 (over y).
Axes of the slice: x: 4, y: 4, z: 8, core: 2. Of those that a mesh axis runs over, the one named last changes fastest.
Arguments:
- kspace: float32 [128, 32768], P('coil', 'rows'), may hold values from -6 to 6
- sample_mask: int32 [128, 32768], P('coil', 'rows'), may hold values 0 or 1
- start_basis: float32 [4, 2048, 128], P('coil', 'rows'), may hold values from -6 to 6
Outputs:
- recovered: float32 [128, 32768], P('coil', 'rows')
- basis: float32 [4, 2048, 128], P('coil', 'rows')
The draws below stay inside these ranges and needn't reach their ends.
All inputs are finite; a program needn't handle non-finite values. No bound on the sum of `sample_mask` on one device may be relied on, other than what follows from the above.
Results may differ from the reference program's by a relative error of at most 0.00011.
Values sent between devices are 32-bit elements; how exact they have to be, the bound alone decides.
A program may use at most 64 MiB of HBM per device.

```python
import jax
import jax.numpy as jnp
from jax import lax

KER = 64
CH = 128
RANK = 128
ITERS = 2
TILE_DEV = 512
POS = 32768
GROUPS = 4
CHG = 32
GW = 2048
N_ROWS = 64


def with_ends(drawn, key, smallest, largest):
    shape = drawn.shape
    index_at = [jax.random.randint(jax.random.fold_in(key, axis), (), 0, shape[axis]) for axis in range(len(shape))]
    drawn = drawn.at[tuple(index_at)].set(smallest)
    longest = shape.index(max(shape))
    index_at[longest] = (index_at[longest] + 1) % shape[longest]
    return drawn.at[tuple(index_at)].set(largest)


def block_scale(rng, dims, shards, low, high):
    def one(axis_at, blocks):
        heights = jax.random.uniform(jax.random.fold_in(jax.random.fold_in(rng, 6), axis_at), (blocks,), jnp.float32, low / len(shards), high / len(shards))
        return jnp.repeat(jnp.exp(heights), dims[axis_at] // blocks).reshape((-1,) + (1,) * (len(dims) - axis_at - 1))

    gain = one(*shards[0])
    for cut in shards[1:]:
        gain = gain * one(*cut)
    return gain


def bell_draw(stream_key, extent, deviation, bound, pieces=(), kind=jnp.bfloat16):
    level = block_scale(stream_key, extent, pieces, -0.22, 0.18) if pieces else 1.0
    array = jax.random.normal(stream_key, extent, jnp.float32) * deviation * level
    return jnp.minimum(jnp.maximum(array, -bound), bound).astype(kind)


def setup_inputs(seed: int = 0) -> dict:
    key_list = jax.random.split(jax.random.key(seed), 4)
    kspace = bell_draw(key_list[0], (CH, POS), 1.0, 6.0, ((0, 4), (1, 64)), jnp.float32)
    sample_mask = with_ends((jax.random.randint(key_list[1], (CH, POS), 0, 2) < 1).astype(jnp.int32), jax.random.fold_in(key_list[1], 1), 0, 1)
    start_basis = bell_draw(key_list[2], (GROUPS, GW, RANK), 1.0, 6.0, ((0, 4), (1, 64)), jnp.float32)
    return dict(kspace=kspace, sample_mask=sample_mask, start_basis=start_basis)


threshold = 0.05

def hankel_block(extended, block_index):
    window = lax.dynamic_slice_in_dim(extended, block_index * TILE_DEV, TILE_DEV + KER - 1, 0)
    shifted = jnp.stack([window[offset:offset + TILE_DEV] for offset in range(KER)], axis=1)
    shifted = shifted.reshape(TILE_DEV, KER, GROUPS, CHG).transpose(0, 2, 1, 3)
    return shifted.reshape(TILE_DEV, GROUPS * GW)

def reference(kspace, sample_mask, start_basis):
    highest = lax.Precision.HIGHEST
    kspace_rows = kspace.T
    mask_rows = sample_mask.T.astype(jnp.float32)
    sampled = kspace_rows * mask_rows
    extended = jnp.concatenate([sampled, sampled[:KER - 1]], axis=0)
    blocks = jnp.arange(N_ROWS, dtype=jnp.int32)
    basis_now = start_basis.reshape(GROUPS * GW, RANK)
    for iteration in range(ITERS):

        def image_block(block_index):
            return jnp.dot(hankel_block(extended, block_index).astype(jnp.float32), basis_now.astype(jnp.float32), precision=highest, preferred_element_type=jnp.float32)
        images = lax.map(image_block, blocks)

        def add_block(running, block_index):
            hankel_rows = hankel_block(extended, block_index)
            term = lax.dot_general(hankel_rows.astype(jnp.float32), images[block_index].astype(jnp.float32), (((0,), (0,)), ((), ())), precision=highest, preferred_element_type=jnp.float32)
            return (running + term, None)
        normal_whole, unused = lax.scan(add_block, jnp.zeros((GROUPS * GW, RANK), jnp.float32), blocks)
        gram_matrix = jnp.dot(normal_whole.T.astype(jnp.float32), normal_whole.astype(jnp.float32), precision=highest, preferred_element_type=jnp.float32)
        factor = jnp.linalg.cholesky(gram_matrix)
        basis_now = lax.linalg.triangular_solve(factor, normal_whole, left_side=False, lower=True, transpose_a=True)

    def spread_block(block_index):
        images = jnp.dot(hankel_block(extended, block_index).astype(jnp.float32), basis_now.astype(jnp.float32), precision=highest, preferred_element_type=jnp.float32)
        projected = jnp.dot(images.astype(jnp.float32), basis_now.T.astype(jnp.float32), precision=highest, preferred_element_type=jnp.float32)
        stacked = projected.reshape(TILE_DEV, GROUPS, KER, CHG).transpose(0, 2, 1, 3).reshape(TILE_DEV, KER, CH)
        spread = jnp.zeros((TILE_DEV + KER - 1, CH), jnp.float32)
        for offset in range(KER):
            spread = spread.at[offset:offset + TILE_DEV].add(stacked[:, offset])
        return spread
    spreads = lax.map(spread_block, blocks)
    main_part = spreads[:, :TILE_DEV]
    tail_parts = spreads[:, TILE_DEV:]
    previous = jnp.roll(tail_parts, 1, axis=0)
    main_part = main_part.at[:, :KER - 1].add(previous)
    estimate = main_part.reshape(POS, CH) / KER
    residual = mask_rows * (kspace_rows - estimate)
    recovered = estimate + residual - jnp.clip(residual, -threshold, threshold)
    return (recovered.T, basis_now.reshape(GROUPS, GW, RANK))
```

```python
import functools

import jax
import jax.numpy as jnp
from jax import lax
from jax.experimental import pallas as pl
from jax.experimental.pallas import tpu as pltpu
from jax.sharding import PartitionSpec as P

NZ, NX, NY = 8, 4, 4
ITERS = 2
CHG = 32
HALF = 512
RB = 16
THRESHOLD = 0.05
MESH = pl.DeviceIdType.MESH
HIGHEST = lax.Precision.HIGHEST
F32 = jnp.float32
BF16 = jnp.bfloat16
PAD = 128
SEMS = 176


def split(value):
    high = value.astype(BF16)
    return high, (value - high.astype(F32)).astype(BF16)


def mm(a, b, dims=((1,), (0,))):
    return lax.dot_general(a, b, (dims, ((), ())), preferred_element_type=F32)


def exact(a, b, dims=((1,), (0,))):
    return lax.dot_general(
        a, b, (dims, ((), ())), precision=HIGHEST, preferred_element_type=F32
    )


def near_first(n):
    return sorted(range(1, n), key=lambda k: min(k, n - k))


def kernel(
    ks_ref, mask_ref, basis_ref, rec_ref, bout_ref,
    own, sb, edge, halo, bt, vx, vo, vall, s3, s2t, ubuf, yh, yl,
    zp, rx, zs, rz, zo, pz, gz, gx, gp, aug, fac, vfull, ep, er, es, ey,
    send, recv,
):
    tiles = NZ * NX
    ch = NY * CHG
    width = 2 * HALF + 2 * PAD
    blocks = 2 * NY
    rank = blocks * RB
    rows = lax.axis_index("rows")
    y = lax.axis_index("coil")
    core = lax.rem(rows, 2)
    t = lax.div(rows, 2)
    x = lax.rem(t, NX)
    z = lax.div(t, NX)
    b = y * 2 + core
    used = [0]

    def dev(tile, c, yy):
        return (tile * 2 + c, yy)

    def slot():
        used[0] += 1
        return used[0] - 1

    def start(src, dst, device, i, j=None):
        copy = pltpu.make_async_remote_copy(
            src_ref=src, dst_ref=dst, send_sem=send.at[i],
            recv_sem=recv.at[i if j is None else j],
            device_id=device, device_id_type=MESH,
        )
        copy.start()
        return copy

    def arrived(dst, i):
        pltpu.make_async_remote_copy(
            src_ref=dst, dst_ref=dst, send_sem=send.at[i], recv_sem=recv.at[i],
            device_id=(rows, y), device_id_type=MESH,
        ).wait_recv()

    def at(zz, xx):
        return zz * NX + xx

    def plus(v, k, n):
        return lax.rem(v + k, n)

    ring = [(dy, dc) for dy in (0, 1, 3, 2) if dy < NY for dc in range(2)]
    peers = [p for p in ring if p != (0, 0)]
    before, after = plus(t, tiles - 1, tiles), plus(t, 1, tiles)

    barrier = pltpu.get_barrier_semaphore()
    greeted = 0
    for k in range(1, NZ):
        pl.semaphore_signal(barrier, inc=1, device_id=dev(at(plus(z, k, NZ), x), core, y), device_id_type=MESH)
        greeted += 1
    for k in range(1, NX):
        pl.semaphore_signal(barrier, inc=1, device_id=dev(at(z, plus(x, k, NX)), core, y), device_id_type=MESH)
        greeted += 1
    for dy, dc in peers:
        pl.semaphore_signal(barrier, inc=1, device_id=dev(t, plus(core, dc, 2), plus(y, dy, NY)), device_id_type=MESH)
        greeted += 1
    for tile in (before, after):
        for dy, dc in ring:
            pl.semaphore_signal(barrier, inc=1, device_id=dev(tile, plus(core, dc, 2), plus(y, dy, NY)), device_id_type=MESH)
            greeted += 1
    lanes = lax.broadcasted_iota(jnp.int32, (rank, ch), 1)
    tiled = jnp.concatenate([basis_ref[...]] * NY, axis=0).T
    placed = jnp.where(lax.div(lanes, CHG) == y, tiled, 0.0)
    bt[...] = placed.reshape(blocks, RB, ch)
    sampled = ks_ref[...] * mask_ref[...].astype(F32)
    own[...] = sampled
    edge[...] = jnp.where(core == 0, sampled[:, :PAD], sampled[:, HALF - PAD:])
    pl.semaphore_wait(barrier, greeted)

    waiting = []
    basis_in = []
    for dy, dc in peers:
        i = slot()
        yy, cc = plus(y, dy, NY), plus(core, dc, 2)
        waiting.append(start(bt.at[yy * 2 + cc], vx.at[core, y], dev(t, cc, yy), i))
        basis_in.append((plus(core, dc, 2), plus(y, NY - dy, NY), i))
    tile_in = []
    for dy, dc in peers:
        i = slot()
        yy, cc = plus(y, dy, NY), plus(core, dc, 2)
        waiting.append(start(own, sb.at[core, y], dev(t, cc, yy), i))
        tile_in.append((plus(core, dc, 2), plus(y, NY - dy, NY), i))
    halo_base = [slot() for _ in range(2 * NY)]
    target = lax.rem(t + tiles + 2 * core - 1, tiles)
    for dy, dc in ring:
        i = halo_base[dc * NY + dy]
        yy, cc = plus(y, dy, NY), plus(core, dc, 2)
        waiting.append(start(edge, halo.at[core, y], dev(target, cc, yy), i, halo_base[0] + core * NY + dy))
    vx[core, y] = bt[b]
    sb[core, y] = own[...]
    for cc, yy, i in basis_in:
        arrived(vx.at[cc, yy], i)
    for half in range(2):
        total = vx[half, 0]
        for yy in range(1, NY):
            total = total + vx[half, yy]
        vo[:, half * ch:(half + 1) * ch] = total

    def gather_basis():
        vall[t] = vo[...]
        sent = []
        order = near_first(NZ)
        first = {}
        for k in reversed(order):
            first[k] = slot()
            sent.append(start(vall.at[t], vall.at[t], dev(at(plus(z, k, NZ), x), core, y), first[k]))
        second = []
        for k in [0] + order:
            here = at(plus(z, NZ - k, NZ), x)
            if k:
                arrived(vall.at[here], first[k])
            for q in range(1, NX):
                i = slot()
                sent.append(start(vall.at[here], vall.at[here], dev(at(z, plus(x, q, NX)), core, y), i))
                second.append((at(plus(z, NZ - k, NZ), plus(x, NX - q, NX)), i))
        return sent, second

    def finish_gather(sent, second):
        for here, i in second:
            arrived(vall.at[here], i)
        for copy in sent:
            copy.wait_send()

    def analyse(store):
        for m in range(4):
            per = tiles // 4
            part = vall[m * per:(m + 1) * per].reshape(per * RB, 2 * ch)
            high, low = split(part)
            ubuf[m * per * RB:(m + 1) * per * RB, :] = mm(
                jnp.concatenate([high, high, low], axis=1), s3[...]
            )
        image = ubuf[0:RB, :]
        for i in range(1, tiles):
            image = image + pltpu.roll(ubuf[i * RB:(i + 1) * RB, :], width - 2 * i, 1)
        place = lax.broadcasted_iota(jnp.int32, (RB, width), 1)
        keep = place < PAD + 2 * HALF
        if store:
            keep = jnp.logical_and(keep, place >= PAD)
        image = jnp.where(keep, image, 0.0)
        for i in range(tiles):
            moved = image if i == 0 else pltpu.roll(image, 2 * i, 1)
            high, low = split(moved)
            yh[i * RB:(i + 1) * RB, :] = high
            yl[i * RB:(i + 1) * RB, :] = low

    def setup_tile():
        for cc, yy, i in tile_in:
            arrived(sb.at[cc, yy], i)
        for s in range(2):
            for dy in range(NY):
                arrived(halo.at[s, plus(y, NY - dy, NY)], halo_base[s * NY + dy])
        full = jnp.concatenate(
            [
                jnp.concatenate([halo[1, g], sb[0, g], sb[1, g], halo[0, g]], axis=1)
                for g in range(NY)
            ],
            axis=0,
        )
        pair = jnp.concatenate([full, pltpu.roll(full, width - 1, 1)], axis=0)
        high, low = split(pair)
        s3[0:2 * ch, :] = high
        s3[2 * ch:4 * ch, :] = low
        s3[4 * ch:6 * ch, :] = high
        turned_high, turned_low = split(pair.T)
        s2t[:, 0:2 * ch] = turned_high
        s2t[:, 2 * ch:4 * ch] = turned_low

    def normal_sum():
        per = tiles // 4
        for m in range(4):
            at_rows = slice(m * per * RB, (m + 1) * per * RB)
            high, low = yh[at_rows, :], yl[at_rows, :]
            main = s2t[:, 0:2 * ch]
            part = mm(high, main) + mm(low, main) + mm(high, s2t[:, 2 * ch:4 * ch])
            zp[m * per:(m + 1) * per] = part.reshape(per, RB, 2 * ch)
        sent = []
        order = near_first(NZ)[::-1] + [0]
        posts = []
        for o, k in enumerate(order):
            for q in range(1, NX):
                i = slot()
                xx = plus(x, q, NX)
                sent.append(start(zp.at[at(plus(z, k, NZ), xx)], rx.at[q - 1, o], dev(at(z, xx), core, y), i))
                posts.append(i)
        back = []
        for o, k in enumerate(order):
            for q in range(1, NX):
                arrived(rx.at[q - 1, o], posts[o * (NX - 1) + q - 1])
            total = zp[at(plus(z, k, NZ), x)]
            for q in range(1, NX):
                total = total + rx[q - 1, o]
            if k:
                zs[o] = total
                i = slot()
                sent.append(start(zs.at[o], rz.at[o], dev(at(plus(z, k, NZ), x), core, y), i))
                back.append((o, i))
            else:
                mine = total
        for o, i in back:
            arrived(rz.at[o], i)
            mine = mine + rz[o]
        zo[...] = mine
        return sent

    def exchange(src, ref_of, sent):
        posts = []
        for dy, dc in peers[::-1]:
            i = slot()
            yy, cc = plus(y, dy, NY), plus(core, dc, 2)
            sent.append(start(src, ref_of(b), dev(t, cc, yy), i))
            posts.append((plus(y, NY - dy, NY) * 2 + plus(core, dc, 2), i))
        for bb, i in posts[::-1]:
            arrived(ref_of(bb), i)

    def gram_sum(it, sent):
        pz[it, b] = zo[...]
        exchange(zo, lambda bb: pz.at[it, bb], sent)
        gathered = pz[it].reshape(rank, 2 * ch)
        gz[z] = exact(zo[...], gathered, ((1,), (1,)))
        posts = []
        for k in near_first(NZ)[::-1]:
            i = slot()
            sent.append(start(gz.at[z], gz.at[z], dev(at(plus(z, k, NZ), x), core, y), i))
            posts.append((plus(z, NZ - k, NZ), i))
        for zz, i in posts[::-1]:
            arrived(gz.at[zz], i)
        total = gz[0]
        for k in range(1, NZ):
            total = total + gz[k]
        gx[x] = total
        posts = []
        for k in near_first(NX)[::-1]:
            i = slot()
            sent.append(start(gx.at[x], gx.at[x], dev(at(z, plus(x, k, NX)), core, y), i))
            posts.append((plus(x, NX - k, NX), i))
        for xx, i in posts[::-1]:
            arrived(gx.at[xx], i)
        total = gx[0]
        for k in range(1, NX):
            total = total + gx[k]
        gp[b] = total
        exchange(gp.at[b], lambda bb: gp.at[bb], sent)
        return gathered

    def inverse_factor():
        line = lax.broadcasted_iota(jnp.int32, (rank, rank), 0)
        column = lax.broadcasted_iota(jnp.int32, (rank, rank), 1)
        aug[:, :rank] = gp[...].reshape(rank, rank)
        aug[:, rank:] = jnp.where(line == column, 1.0, 0.0).astype(F32)
        sub = lax.broadcasted_iota(jnp.int32, (8, rank), 0)

        def panel(k, carry):
            top = pl.multiple_of(k * 8, 8)
            left = aug[pl.ds(top, 8), :rank]
            right = aug[pl.ds(top, 8), rank:]
            turned = pltpu.roll(left, lax.rem(rank - k * 8, rank), 1)
            cols = [jnp.broadcast_to(turned[:, q:q + 1], (8, rank)) for q in range(8)]
            scale = jnp.zeros((8, rank), F32)
            for p in range(8):
                inverse_root = lax.rsqrt(jnp.broadcast_to(cols[p][p:p + 1, :], (8, rank)))
                step = jnp.where(sub > p, cols[p] * inverse_root * inverse_root, 0.0)
                scale = jnp.where(sub == p, inverse_root, scale)
                for q in range(p + 1, 8):
                    cols[q] = cols[q] - step * jnp.broadcast_to(cols[q][p:p + 1, :], (8, rank))
                left = left - step * jnp.broadcast_to(left[p:p + 1, :], (8, rank))
                right = right - step * jnp.broadcast_to(right[p:p + 1, :], (8, rank))
            both = jnp.concatenate([left * scale, right * scale], axis=1)
            fac[pl.ds(top, 8), :] = both[:, rank:]
            aug[...] = aug[...] - exact(both[:, :rank], both, ((0,), (0,)))
            return carry

        lax.fori_loop(0, rank // 8, panel, 0)

    def iteration(it, carry):
        sent, second = gather_basis()
        finish_gather(sent, second)
        analyse(True)
        sent = normal_sum()
        gathered = gram_sum(it, sent)
        inverse_factor()
        vfull[...] = exact(fac[...], gathered).reshape(blocks, RB, 2 * ch)
        for copy in sent:
            copy.wait_send()
        vo[...] = vfull[b]
        return carry

    setup_tile()
    lax.fori_loop(0, ITERS, iteration, 0)
    sent, second = gather_basis()
    finish_gather(sent, second)
    both = vfull[...].reshape(rank, 2 * ch)
    aug[:, :rank] = jnp.where(core == 0, both[:, :ch], both[:, ch:]).T
    bout_ref[...] = aug[pl.ds(pl.multiple_of(y * CHG, CHG), CHG), :rank]

    analyse(False)
    turned_high, turned_low = split(vall[...].reshape(tiles * RB, 2 * ch).T)
    for bit in range(2):
        at_rows = slice(bit * ch, (bit + 1) * ch)
        part = (
            mm(turned_high[at_rows], yh[...])
            + mm(turned_low[at_rows], yh[...])
            + mm(turned_high[at_rows], yl[...])
        )
        if bit:
            total = total + pltpu.roll(part, 1, 1)
        else:
            total = part
    for half in range(2):
        piece = total[:, PAD + half * HALF:PAD + (half + 1) * HALF]
        ep[half] = piece.reshape(NY, CHG, HALF)
    sent = []
    other = 1 - core
    order = near_first(NY)[::-1] + [0]
    posts = []
    for dy in order:
        i = slot()
        yy = plus(y, dy, NY)
        sent.append(start(ep.at[other, yy], er.at[yy], dev(t, other, y), i))
        posts.append(i)
    back = []
    for dy, i in zip(order, posts):
        yy = plus(y, dy, NY)
        arrived(er.at[yy], i)
        piece = ep[core, yy] + er[yy]
        if dy:
            es[dy] = piece
            j = slot()
            sent.append(start(es.at[dy], ey.at[dy], dev(t, core, yy), j))
            back.append((dy, j))
        else:
            estimate = piece
    for dy, j in back:
        arrived(ey.at[dy], j)
        estimate = estimate + ey[dy]
    estimate = estimate * (1.0 / (2 * tiles))
    residual = mask_ref[...].astype(F32) * (ks_ref[...] - estimate)
    rec_ref[...] = estimate + residual - jnp.clip(residual, -THRESHOLD, THRESHOLD)
    for copy in sent + waiting:
        copy.wait_send()
    assert used[0] <= SEMS, used[0]


def shards(kspace, sample_mask, start_basis):
    tiles = NZ * NX
    ch = NY * CHG
    width = 2 * HALF + 2 * PAD
    blocks = 2 * NY
    rank = blocks * RB
    vmem = pltpu.VMEM
    recovered, basis = pl.pallas_call(
        kernel,
        out_shape=(
            jax.ShapeDtypeStruct((CHG, HALF), F32),
            jax.ShapeDtypeStruct((CHG, rank), F32),
        ),
        in_specs=[pl.BlockSpec(memory_space=pltpu.VMEM)] * 3,
        out_specs=(pl.BlockSpec(memory_space=pltpu.VMEM),) * 2,
        scratch_shapes=[
            vmem((CHG, HALF), F32),
            vmem((2, NY, CHG, HALF), F32),
            vmem((CHG, PAD), F32),
            vmem((2, NY, CHG, PAD), F32),
            vmem((blocks, RB, ch), F32),
            vmem((2, NY, RB, ch), F32),
            vmem((RB, 2 * ch), F32),
            vmem((tiles, RB, 2 * ch), F32),
            vmem((6 * ch, width), BF16),
            vmem((width, 4 * ch), BF16),
            vmem((tiles * RB, width), F32),
            vmem((tiles * RB, width), BF16),
            vmem((tiles * RB, width), BF16),
            vmem((tiles, RB, 2 * ch), F32),
            vmem((max(NX - 1, 1), NZ, RB, 2 * ch), F32),
            vmem((NZ, RB, 2 * ch), F32),
            vmem((NZ, RB, 2 * ch), F32),
            vmem((RB, 2 * ch), F32),
            vmem((ITERS, blocks, RB, 2 * ch), F32),
            vmem((NZ, RB, rank), F32),
            vmem((NX, RB, rank), F32),
            vmem((blocks, RB, rank), F32),
            vmem((rank, 2 * rank), F32),
            vmem((rank, rank), F32),
            vmem((blocks, RB, 2 * ch), F32),
            vmem((2, NY, CHG, HALF), F32),
            vmem((NY, CHG, HALF), F32),
            vmem((NY, CHG, HALF), F32),
            vmem((NY, CHG, HALF), F32),
            pltpu.SemaphoreType.DMA((SEMS,)),
            pltpu.SemaphoreType.DMA((SEMS,)),
        ],
        compiler_params=pltpu.CompilerParams(
            collective_id=0, has_side_effects=True, vmem_limit_bytes=48 << 20
        ),
    )(kspace, sample_mask, start_basis.reshape(CHG, rank))
    return recovered, basis.reshape(1, CHG, rank)


def solution(mesh):
    return jax.shard_map(
        shards,
        mesh=mesh,
        in_specs=(P("coil", "rows"), P("coil", "rows"), P("coil", "rows", None)),
        out_specs=(P("coil", "rows"), P("coil", "rows", None)),
        check_vma=False,
    )
```

```python
import functools

import jax
import jax.numpy as jnp
from jax import lax
from jax.experimental import pallas as pl
from jax.experimental.pallas import tpu as pltpu
from jax.sharding import PartitionSpec as P

NZ, NX, NY = 8, 4, 4
ITERS = 2
CHG = 32
HALF = 512
RB = 16
THRESHOLD = 0.05
MESH = pl.DeviceIdType.MESH
HIGHEST = lax.Precision.HIGHEST
F32 = jnp.float32
BF16 = jnp.bfloat16
PAD = 128
SEMS = 256


def split(value):
    high = value.astype(BF16)
    return high, (value - high.astype(F32)).astype(BF16)


def mm(a, b, dims=((1,), (0,))):
    return lax.dot_general(a, b, (dims, ((), ())), preferred_element_type=F32)


def exact(a, b, dims=((1,), (0,))):
    return lax.dot_general(
        a, b, (dims, ((), ())), precision=HIGHEST, preferred_element_type=F32
    )


def near_first(n):
    return sorted(range(1, n), key=lambda k: min(k, n - k))


def kernel(
    ks_ref, mask_ref, basis_ref, rec_ref, bout_ref,
    own, sb, edge, halo, bt, vx, vall, s3, s2t, ubuf, yh, yl,
    zp, rx, zs, rz, pz, gz, gx, gp, aug, fac, vfull, yx, ep, er, es, ey,
    send, recv,
):
    tiles = NZ * NX
    ch = NY * CHG
    width = 2 * HALF + 2 * PAD
    blocks = 2 * NY
    rank = blocks * RB
    rows = lax.axis_index("rows")
    y = lax.axis_index("coil")
    core = lax.rem(rows, 2)
    t = lax.div(rows, 2)
    x = lax.rem(t, NX)
    z = lax.div(t, NX)
    b = y * 2 + core
    used = [0]

    def dev(tile, c, yy):
        return (tile * 2 + c, yy)

    def slot():
        used[0] += 1
        return used[0] - 1

    def start(src, dst, device, i, j=None):
        copy = pltpu.make_async_remote_copy(
            src_ref=src, dst_ref=dst, send_sem=send.at[i],
            recv_sem=recv.at[i if j is None else j],
            device_id=device, device_id_type=MESH,
        )
        copy.start()
        return copy

    def arrived(dst, i):
        pltpu.make_async_remote_copy(
            src_ref=dst, dst_ref=dst, send_sem=send.at[i], recv_sem=recv.at[i],
            device_id=(rows, y), device_id_type=MESH,
        ).wait_recv()

    def at(zz, xx):
        return zz * NX + xx

    def plus(v, k, n):
        return lax.rem(v + k, n)

    ring = [(dy, dc) for dy in (0, 1, 3, 2) if dy < NY for dc in range(2)]
    peers = [p for p in ring if p != (0, 0)]
    before, after = plus(t, tiles - 1, tiles), plus(t, 1, tiles)

    barrier = pltpu.get_barrier_semaphore()
    greeted = 0
    for k in range(1, NZ):
        pl.semaphore_signal(barrier, inc=1, device_id=dev(at(plus(z, k, NZ), x), core, y), device_id_type=MESH)
        greeted += 1
    for k in range(1, NX):
        pl.semaphore_signal(barrier, inc=1, device_id=dev(at(z, plus(x, k, NX)), core, y), device_id_type=MESH)
        greeted += 1
    for dy, dc in peers:
        pl.semaphore_signal(barrier, inc=1, device_id=dev(t, plus(core, dc, 2), plus(y, dy, NY)), device_id_type=MESH)
        greeted += 1
    for tile in (before, after):
        for dy, dc in ring:
            pl.semaphore_signal(barrier, inc=1, device_id=dev(tile, plus(core, dc, 2), plus(y, dy, NY)), device_id_type=MESH)
            greeted += 1
    lanes = lax.broadcasted_iota(jnp.int32, (rank, ch), 1)
    tiled = jnp.concatenate([basis_ref[...]] * NY, axis=0).T
    placed = jnp.where(lax.div(lanes, CHG) == y, tiled, 0.0)
    bt[...] = placed.reshape(blocks, RB, ch)
    sampled = ks_ref[...] * mask_ref[...].astype(F32)
    own[...] = sampled
    edge[...] = jnp.where(core == 0, sampled[:, :PAD], sampled[:, HALF - PAD:])
    pl.semaphore_wait(barrier, greeted)

    waiting = []
    basis_in = []
    for dy, dc in peers:
        i = slot()
        yy, cc = plus(y, dy, NY), plus(core, dc, 2)
        waiting.append(start(bt.at[yy * 2 + cc], vx.at[core, y], dev(t, cc, yy), i))
        basis_in.append((plus(core, dc, 2), plus(y, NY - dy, NY), i))
    tile_in = []
    for dy, dc in peers:
        i = slot()
        yy, cc = plus(y, dy, NY), plus(core, dc, 2)
        waiting.append(start(own, sb.at[core, y], dev(t, cc, yy), i))
        tile_in.append((plus(core, dc, 2), plus(y, NY - dy, NY), i))
    halo_base = [slot() for _ in range(2 * NY)]
    target = lax.rem(t + tiles + 2 * core - 1, tiles)
    for dy, dc in ring:
        i = halo_base[dc * NY + dy]
        yy, cc = plus(y, dy, NY), plus(core, dc, 2)
        waiting.append(start(edge, halo.at[core, y], dev(target, cc, yy), i, halo_base[0] + core * NY + dy))
    vx[core, y] = bt[b]
    sb[core, y] = own[...]
    for cc, yy, i in basis_in:
        arrived(vx.at[cc, yy], i)
    halves = []
    for half in range(2):
        total = vx[half, 0]
        for yy in range(1, NY):
            total = total + vx[half, yy]
        halves.append(total)
    first_chunk = jnp.concatenate(halves, axis=1)

    pending = []

    def gather_start(it, chunk):
        vall[it, t] = chunk
        first = {}
        for k in near_first(NZ)[::-1]:
            first[k] = slot()
            pending.append(start(vall.at[it, t], vall.at[it, t], dev(at(plus(z, k, NZ), x), core, y), first[k]))
        second = []
        gather_relay((it, first, second), (0,))
        return it, first, second

    def gather_relay(state, steps):
        it, first, second = state
        for k in steps:
            zz = plus(z, NZ - k, NZ)
            here = at(zz, x)
            if k:
                arrived(vall.at[it, here], first[k])
            for q in range(1, NX):
                i = slot()
                pending.append(start(vall.at[it, here], vall.at[it, here], dev(at(z, plus(x, q, NX)), core, y), i))
                second.append((at(zz, plus(x, NX - q, NX)), i))

    def gather_finish(state):
        for here, i in state[2]:
            arrived(vall.at[state[0], here], i)

    def analyse(it):
        per = tiles // 4
        for m in range(4):
            part = vall[it, m * per:(m + 1) * per].reshape(per * RB, 2 * ch)
            high, low = split(part)
            ubuf[m * per * RB:(m + 1) * per * RB, :] = mm(
                jnp.concatenate([high, high, low], axis=1), s3[...]
            )
        image = ubuf[0:RB, :]
        for i in range(1, tiles):
            image = image + pltpu.roll(ubuf[i * RB:(i + 1) * RB, :], width - 2 * i, 1)
        return image

    def spread(image):
        for i in range(tiles):
            moved = image if i == 0 else pltpu.roll(image, 2 * i, 1)
            high, low = split(moved)
            yh[i * RB:(i + 1) * RB, :] = high
            yl[i * RB:(i + 1) * RB, :] = low

    def setup_tile():
        for cc, yy, i in tile_in:
            arrived(sb.at[cc, yy], i)
        for s in range(2):
            for dy in range(NY):
                arrived(halo.at[s, plus(y, NY - dy, NY)], halo_base[s * NY + dy])
        full = jnp.concatenate(
            [
                jnp.concatenate([halo[1, g], sb[0, g], sb[1, g], halo[0, g]], axis=1)
                for g in range(NY)
            ],
            axis=0,
        )
        pair = jnp.concatenate([full, pltpu.roll(full, width - 1, 1)], axis=0)
        high, low = split(pair)
        s3[0:2 * ch, :] = high
        s3[2 * ch:4 * ch, :] = low
        s3[4 * ch:6 * ch, :] = high
        turned_high, turned_low = split(pair.T)
        s2t[:, 0:2 * ch] = turned_high
        s2t[:, 2 * ch:4 * ch] = turned_low

    far_first = near_first(NZ)[::-1] + [0]

    def normal_start(it, image):
        place = lax.broadcasted_iota(jnp.int32, (RB, width), 1)
        spread(jnp.where(jnp.logical_and(place >= PAD, place < PAD + 2 * HALF), image, 0.0))
        per = tiles // 4
        for m in range(4):
            at_rows = slice(m * per * RB, (m + 1) * per * RB)
            high, low = yh[at_rows, :], yl[at_rows, :]
            main = s2t[:, 0:2 * ch]
            part = mm(high, main) + mm(low, main) + mm(high, s2t[:, 2 * ch:4 * ch])
            zp[it, m * per:(m + 1) * per] = part.reshape(per, RB, 2 * ch)
        posts = []
        for o, k in enumerate(far_first):
            for q in range(1, NX):
                i = slot()
                xx = plus(x, q, NX)
                pending.append(start(zp.at[it, at(plus(z, k, NZ), xx)], rx.at[it, q - 1, o], dev(at(z, xx), core, y), i))
                posts.append(i)
        return it, posts, []

    def normal_relay(state, o):
        it, posts, back = state
        k = far_first[o]
        for q in range(1, NX):
            arrived(rx.at[it, q - 1, o], posts[o * (NX - 1) + q - 1])
        total = zp[it, at(plus(z, k, NZ), x)]
        for q in range(1, NX):
            total = total + rx[it, q - 1, o]
        zs[it, o] = total
        if k:
            i = slot()
            pending.append(start(zs.at[it, o], rz.at[it, o], dev(at(plus(z, k, NZ), x), core, y), i))
            back.append((o, i))

    def normal_finish(state):
        it, _, back = state
        mine = zs[it, NZ - 1]
        for o, i in back:
            arrived(rz.at[it, o], i)
            mine = mine + rz[it, o]
        return mine

    def share(src, ref_of):
        posts = []
        for dy, dc in peers[::-1]:
            i = slot()
            yy, cc = plus(y, dy, NY), plus(core, dc, 2)
            pending.append(start(src, ref_of(b), dev(t, cc, yy), i))
            posts.append((plus(y, NY - dy, NY) * 2 + plus(core, dc, 2), i))
        return ref_of, posts

    def shared(state):
        ref_of, posts = state
        for bb, i in posts[::-1]:
            arrived(ref_of(bb), i)

    def rows_share(it, chunk):
        pz[it, b] = chunk
        return share(pz.at[it, b], lambda bb: pz.at[it, bb])

    def along_z(it, product):
        gz[it, z] = product
        posts = []
        for k in near_first(NZ)[::-1]:
            i = slot()
            pending.append(start(gz.at[it, z], gz.at[it, z], dev(at(plus(z, k, NZ), x), core, y), i))
            posts.append((plus(z, NZ - k, NZ), i))
        return it, posts

    def along_x(state):
        it, posts = state
        for zz, i in posts[::-1]:
            arrived(gz.at[it, zz], i)
        total = gz[it, 0]
        for k in range(1, NZ):
            total = total + gz[it, k]
        gx[it, x] = total
        posts = []
        for k in near_first(NX)[::-1]:
            i = slot()
            pending.append(start(gx.at[it, x], gx.at[it, x], dev(at(z, plus(x, k, NX)), core, y), i))
            posts.append((plus(x, NX - k, NX), i))
        return it, posts

    def gram_share(state):
        it, posts = state
        for xx, i in posts[::-1]:
            arrived(gx.at[it, xx], i)
        total = gx[it, 0]
        for k in range(1, NX):
            total = total + gx[it, k]
        gp[it, b] = total
        return share(gp.at[it, b], lambda bb: gp.at[it, bb])

    def factor_start(it):
        line = lax.broadcasted_iota(jnp.int32, (rank, rank), 0)
        column = lax.broadcasted_iota(jnp.int32, (rank, rank), 1)
        aug[:, :rank] = gp[it].reshape(rank, rank)
        aug[:, rank:] = jnp.where(line == column, 1.0, 0.0).astype(F32)

    def factor_panels(it, low, high):
        sub = lax.broadcasted_iota(jnp.int32, (8, rank), 0)

        def panel(k, carry):
            top = pl.multiple_of(k * 8, 8)
            left = aug[pl.ds(top, 8), :rank]
            right = aug[pl.ds(top, 8), rank:]
            turned = pltpu.roll(left, lax.rem(rank - k * 8, rank), 1)
            cols = [jnp.broadcast_to(turned[:, q:q + 1], (8, rank)) for q in range(8)]
            scale = jnp.zeros((8, rank), F32)
            for p in range(8):
                inverse_root = lax.rsqrt(jnp.broadcast_to(cols[p][p:p + 1, :], (8, rank)))
                step = jnp.where(sub > p, cols[p] * inverse_root * inverse_root, 0.0)
                scale = jnp.where(sub == p, inverse_root, scale)
                for q in range(p + 1, 8):
                    cols[q] = cols[q] - step * jnp.broadcast_to(cols[q][p:p + 1, :], (8, rank))
                left = left - step * jnp.broadcast_to(left[p:p + 1, :], (8, rank))
                right = right - step * jnp.broadcast_to(right[p:p + 1, :], (8, rank))
            both = jnp.concatenate([left * scale, right * scale], axis=1)
            fac[it, pl.ds(top, 8), :] = both[:, rank:]
            aug[...] = aug[...] - exact(both[:, :rank], both, ((0,), (0,)))
            return carry

        lax.fori_loop(low, high, panel, 0)

    panels = rank // 8
    order = near_first(NZ)
    moving = gather_start(0, first_chunk)
    setup_tile()
    gather_relay(moving, order)
    gather_finish(moving)
    folding = normal_start(0, analyse(0))
    for o in range(NZ):
        normal_relay(folding, o)
    chunk = normal_finish(folding)

    moving = gather_start(1, chunk)
    joined = rows_share(0, chunk)
    gather_relay(moving, order)
    shared(joined)
    gram = along_z(0, exact(pz[0, b], pz[0].reshape(rank, 2 * ch), ((1,), (1,))))
    gather_finish(moving)
    image = analyse(1)
    gram = along_x(gram)
    folding = normal_start(1, image)
    gram = gram_share(gram)
    head = max(NZ - 5, 1)
    for o in range(head):
        normal_relay(folding, o)
    shared(gram)
    factor_start(0)
    for o in range(head, NZ):
        at_panel = 2 * (o - head)
        factor_panels(0, at_panel, at_panel + 2)
        normal_relay(folding, o)
    factor_panels(0, 2 * (NZ - head), panels)
    chunk = normal_finish(folding)
    joined = rows_share(1, chunk)
    shared(joined)
    vfull[...] = exact(fac[0], pz[1].reshape(rank, 2 * ch)).reshape(blocks, RB, 2 * ch)

    chunk = vfull[b]
    gram = along_z(1, exact(chunk, vfull[...].reshape(rank, 2 * ch), ((1,), (1,))))
    moving = gather_start(2, chunk)
    gather_relay(moving, order[:4])
    gram = along_x(gram)
    gather_relay(moving, order[4:])
    gram = gram_share(gram)
    gather_finish(moving)
    yx[b] = analyse(2)[:, :width - PAD]
    joined = share(yx.at[b], lambda bb: yx.at[bb])
    turned_high, turned_low = split(vall[2].reshape(tiles * RB, 2 * ch).T)
    shared(gram)
    factor_start(1)
    factor_panels(1, 0, panels)
    inverse = fac[1]
    fac[0] = inverse.T
    both = exact(inverse, vfull[...].reshape(rank, 2 * ch))
    aug[:, :rank] = jnp.where(core == 0, both[:, :ch], both[:, ch:]).T
    bout_ref[...] = aug[pl.ds(pl.multiple_of(y * CHG, CHG), CHG), :rank]
    weights = exact(fac[0, pl.ds(pl.multiple_of(b * RB, RB), RB), :], inverse)
    shared(joined)
    image = exact(weights, yx[...].reshape(rank, width - PAD))
    spread(jnp.concatenate([image, jnp.zeros((RB, PAD), F32)], axis=1))
    for bit in range(2):
        at_rows = slice(bit * ch, (bit + 1) * ch)
        part = (
            mm(turned_high[at_rows], yh[...])
            + mm(turned_low[at_rows], yh[...])
            + mm(turned_high[at_rows], yl[...])
        )
        if bit:
            total = total + pltpu.roll(part, 1, 1)
        else:
            total = part
    for half in range(2):
        piece = total[:, PAD + half * HALF:PAD + (half + 1) * HALF]
        ep[half] = piece.reshape(NY, CHG, HALF)
    other = 1 - core
    order = near_first(NY)[::-1] + [0]
    posts = []
    for dy in order:
        i = slot()
        yy = plus(y, dy, NY)
        pending.append(start(ep.at[other, yy], er.at[yy], dev(t, other, y), i))
        posts.append(i)
    back = []
    for dy, i in zip(order, posts):
        yy = plus(y, dy, NY)
        arrived(er.at[yy], i)
        piece = ep[core, yy] + er[yy]
        if dy:
            es[dy] = piece
            j = slot()
            pending.append(start(es.at[dy], ey.at[dy], dev(t, core, yy), j))
            back.append((dy, j))
        else:
            estimate = piece
    for dy, j in back:
        arrived(ey.at[dy], j)
        estimate = estimate + ey[dy]
    estimate = estimate * (1.0 / (2 * tiles))
    residual = mask_ref[...].astype(F32) * (ks_ref[...] - estimate)
    rec_ref[...] = estimate + residual - jnp.clip(residual, -THRESHOLD, THRESHOLD)
    for copy in pending + waiting:
        copy.wait_send()
    assert used[0] <= SEMS, used[0]


def shards(kspace, sample_mask, start_basis):
    tiles = NZ * NX
    ch = NY * CHG
    width = 2 * HALF + 2 * PAD
    blocks = 2 * NY
    rank = blocks * RB
    vmem = pltpu.VMEM
    recovered, basis = pl.pallas_call(
        kernel,
        out_shape=(
            jax.ShapeDtypeStruct((CHG, HALF), F32),
            jax.ShapeDtypeStruct((CHG, rank), F32),
        ),
        in_specs=[pl.BlockSpec(memory_space=pltpu.VMEM)] * 3,
        out_specs=(pl.BlockSpec(memory_space=pltpu.VMEM),) * 2,
        scratch_shapes=[
            vmem((CHG, HALF), F32),
            vmem((2, NY, CHG, HALF), F32),
            vmem((CHG, PAD), F32),
            vmem((2, NY, CHG, PAD), F32),
            vmem((blocks, RB, ch), F32),
            vmem((2, NY, RB, ch), F32),
            vmem((ITERS + 1, tiles, RB, 2 * ch), F32),
            vmem((6 * ch, width), BF16),
            vmem((width, 4 * ch), BF16),
            vmem((tiles * RB, width), F32),
            vmem((tiles * RB, width), BF16),
            vmem((tiles * RB, width), BF16),
            vmem((ITERS, tiles, RB, 2 * ch), F32),
            vmem((ITERS, max(NX - 1, 1), NZ, RB, 2 * ch), F32),
            vmem((ITERS, NZ, RB, 2 * ch), F32),
            vmem((ITERS, NZ, RB, 2 * ch), F32),
            vmem((ITERS, blocks, RB, 2 * ch), F32),
            vmem((ITERS, NZ, RB, rank), F32),
            vmem((ITERS, NX, RB, rank), F32),
            vmem((ITERS, blocks, RB, rank), F32),
            vmem((rank, 2 * rank), F32),
            vmem((ITERS, rank, rank), F32),
            vmem((blocks, RB, 2 * ch), F32),
            vmem((blocks, RB, width - PAD), F32),
            vmem((2, NY, CHG, HALF), F32),
            vmem((NY, CHG, HALF), F32),
            vmem((NY, CHG, HALF), F32),
            vmem((NY, CHG, HALF), F32),
            pltpu.SemaphoreType.DMA((SEMS,)),
            pltpu.SemaphoreType.DMA((SEMS,)),
        ],
        compiler_params=pltpu.CompilerParams(
            collective_id=0, has_side_effects=True, vmem_limit_bytes=48 << 20
        ),
    )(kspace, sample_mask, start_basis.reshape(CHG, rank))
    return recovered, basis.reshape(1, CHG, rank)


def solution(mesh):
    return jax.shard_map(
        shards,
        mesh=mesh,
        in_specs=(P("coil", "rows"), P("coil", "rows"), P("coil", "rows", None)),
        out_specs=(P("coil", "rows"), P("coil", "rows", None)),
        check_vma=False,
    )
```

```python
import functools

import jax
import jax.numpy as jnp
from jax import lax
from jax.experimental import pallas as pl
from jax.experimental.pallas import tpu as pltpu
from jax.sharding import PartitionSpec as P

NZ, NX, NY = 8, 4, 4
ITERS = 2
CHG = 32
HALF = 512
RB = 16
THRESHOLD = 0.05
MESH = pl.DeviceIdType.MESH
HIGHEST = lax.Precision.HIGHEST
F32 = jnp.float32
BF16 = jnp.bfloat16
PAD = 128
PANEL = 16
SEMS = 256


def split(value):
    high = value.astype(BF16)
    return high, (value - high.astype(F32)).astype(BF16)


def mm(a, b, dims=((1,), (0,))):
    return lax.dot_general(a, b, (dims, ((), ())), preferred_element_type=F32)


def exact(a, b, dims=((1,), (0,))):
    return lax.dot_general(
        a, b, (dims, ((), ())), precision=HIGHEST, preferred_element_type=F32
    )


def near_first(n):
    return sorted(range(1, n), key=lambda k: min(k, n - k))


def kernel(
    ks_hbm, mask_hbm, basis_hbm, rec_ref, bout_ref,
    ks_ref, mask_ref, basis_ref, own, sb, edge, halo, bt, vx, vall, s3, s2t, ubuf, yh, yl,
    zp, rx, zs, rz, pz, gz, gx, gp, aug, fac, vfull, yx, ep, er, es, ey,
    send, recv, load,
):
    loads = [
        pltpu.make_async_copy(src, dst, load.at[i])
        for i, (src, dst) in enumerate(
            ((basis_hbm, basis_ref), (ks_hbm, ks_ref), (mask_hbm, mask_ref))
        )
    ]
    for copy in loads:
        copy.start()
    tiles = NZ * NX
    ch = NY * CHG
    width = 2 * HALF + 2 * PAD
    blocks = 2 * NY
    rank = blocks * RB
    rows = lax.axis_index("rows")
    y = lax.axis_index("coil")
    core = lax.rem(rows, 2)
    t = lax.div(rows, 2)
    x = lax.rem(t, NX)
    z = lax.div(t, NX)
    b = y * 2 + core
    used = [0]

    def dev(tile, c, yy):
        return (tile * 2 + c, yy)

    def slot():
        used[0] += 1
        return used[0] - 1

    def start(src, dst, device, i, j=None):
        copy = pltpu.make_async_remote_copy(
            src_ref=src, dst_ref=dst, send_sem=send.at[i],
            recv_sem=recv.at[i if j is None else j],
            device_id=device, device_id_type=MESH,
        )
        copy.start()
        return copy

    def arrived(dst, i):
        pltpu.make_async_remote_copy(
            src_ref=dst, dst_ref=dst, send_sem=send.at[i], recv_sem=recv.at[i],
            device_id=(rows, y), device_id_type=MESH,
        ).wait_recv()

    def at(zz, xx):
        return zz * NX + xx

    def plus(v, k, n):
        return lax.rem(v + k, n)

    ring = [(dy, dc) for dy in (0, 1, 3, 2) if dy < NY for dc in range(2)]
    peers = [p for p in ring if p != (0, 0)]
    before, after = plus(t, tiles - 1, tiles), plus(t, 1, tiles)

    barrier = pltpu.get_barrier_semaphore()
    greeted = 0
    for k in range(1, NZ):
        pl.semaphore_signal(barrier, inc=1, device_id=dev(at(plus(z, k, NZ), x), core, y), device_id_type=MESH)
        greeted += 1
    for k in range(1, NX):
        pl.semaphore_signal(barrier, inc=1, device_id=dev(at(z, plus(x, k, NX)), core, y), device_id_type=MESH)
        greeted += 1
    for dy, dc in peers:
        pl.semaphore_signal(barrier, inc=1, device_id=dev(t, plus(core, dc, 2), plus(y, dy, NY)), device_id_type=MESH)
        greeted += 1
    for tile in (before, after):
        for dy, dc in ring:
            pl.semaphore_signal(barrier, inc=1, device_id=dev(tile, plus(core, dc, 2), plus(y, dy, NY)), device_id_type=MESH)
            greeted += 1
    for copy in loads:
        copy.wait()
    lanes = lax.broadcasted_iota(jnp.int32, (rank, ch), 1)
    tiled = jnp.concatenate([basis_ref[...]] * NY, axis=0).T
    placed = jnp.where(lax.div(lanes, CHG) == y, tiled, 0.0)
    bt[...] = placed.reshape(blocks, RB, ch)
    sampled = ks_ref[...] * mask_ref[...].astype(F32)
    own[...] = sampled
    edge[...] = jnp.where(core == 0, sampled[:, :PAD], sampled[:, HALF - PAD:])
    pl.semaphore_wait(barrier, greeted)

    waiting = []
    basis_in = []
    for dy, dc in peers:
        i = slot()
        yy, cc = plus(y, dy, NY), plus(core, dc, 2)
        waiting.append(start(bt.at[yy * 2 + cc], vx.at[core, y], dev(t, cc, yy), i))
        basis_in.append((plus(core, dc, 2), plus(y, NY - dy, NY), i))
    tile_in = []
    for dy, dc in peers:
        i = slot()
        yy, cc = plus(y, dy, NY), plus(core, dc, 2)
        waiting.append(start(own, sb.at[core, y], dev(t, cc, yy), i))
        tile_in.append((plus(core, dc, 2), plus(y, NY - dy, NY), i))
    halo_base = [slot() for _ in range(2 * NY)]
    target = lax.rem(t + tiles + 2 * core - 1, tiles)
    for dy, dc in ring:
        i = halo_base[dc * NY + dy]
        yy, cc = plus(y, dy, NY), plus(core, dc, 2)
        waiting.append(start(edge, halo.at[core, y], dev(target, cc, yy), i, halo_base[0] + core * NY + dy))
    vx[core, y] = bt[b]
    sb[core, y] = own[...]
    for cc, yy, i in basis_in:
        arrived(vx.at[cc, yy], i)
    halves = []
    for half in range(2):
        total = vx[half, 0]
        for yy in range(1, NY):
            total = total + vx[half, yy]
        halves.append(total)
    first_chunk = jnp.concatenate(halves, axis=1)

    pending = []

    def gather_start(it, chunk):
        vall[it, t] = chunk
        first = {}
        for k in near_first(NZ):
            first[k] = slot()
            pending.append(start(vall.at[it, t], vall.at[it, t], dev(at(plus(z, k, NZ), x), core, y), first[k]))
        second = []
        gather_relay((it, first, second), (0,))
        return it, first, second

    def gather_relay(state, steps):
        it, first, second = state
        for k in steps:
            zz = plus(z, NZ - k, NZ)
            here = at(zz, x)
            if k:
                arrived(vall.at[it, here], first[k])
            for q in range(1, NX):
                i = slot()
                pending.append(start(vall.at[it, here], vall.at[it, here], dev(at(z, plus(x, q, NX)), core, y), i))
                second.append((at(zz, plus(x, NX - q, NX)), i))

    def gather_finish(state, low=0, high=None):
        for here, i in state[2][low:high]:
            arrived(vall.at[state[0], here], i)

    def analyse(it):
        per = tiles // 4
        for m in range(4):
            part = vall[it, m * per:(m + 1) * per].reshape(per * RB, 2 * ch)
            high, low = split(part)
            ubuf[m * per * RB:(m + 1) * per * RB, :] = mm(
                jnp.concatenate([high, high, low], axis=1), s3[...]
            )
        image = ubuf[0:RB, :]
        for i in range(1, tiles):
            image = image + pltpu.roll(ubuf[i * RB:(i + 1) * RB, :], width - 2 * i, 1)
        return image

    def spread(image):
        for i in range(tiles):
            moved = image if i == 0 else pltpu.roll(image, 2 * i, 1)
            high, low = split(moved)
            yh[i * RB:(i + 1) * RB, :] = high
            yl[i * RB:(i + 1) * RB, :] = low

    def setup_tile():
        for cc, yy, i in tile_in:
            arrived(sb.at[cc, yy], i)
        for s in range(2):
            for dy in range(NY):
                arrived(halo.at[s, plus(y, NY - dy, NY)], halo_base[s * NY + dy])
        full = jnp.concatenate(
            [
                jnp.concatenate([halo[1, g], sb[0, g], sb[1, g], halo[0, g]], axis=1)
                for g in range(NY)
            ],
            axis=0,
        )
        pair = jnp.concatenate([full, pltpu.roll(full, width - 1, 1)], axis=0)
        high, low = split(pair)
        s3[0:2 * ch, :] = high
        s3[2 * ch:4 * ch, :] = low
        s3[4 * ch:6 * ch, :] = high
        turned_high, turned_low = split(pair.T)
        s2t[:, 0:2 * ch] = turned_high
        s2t[:, 2 * ch:4 * ch] = turned_low

    far_first = near_first(NZ)[::-1] + [0]

    def normal_start(it, image):
        place = lax.broadcasted_iota(jnp.int32, (RB, width), 1)
        spread(jnp.where(jnp.logical_and(place >= PAD, place < PAD + 2 * HALF), image, 0.0))
        per = tiles // 4
        for m in range(4):
            at_rows = slice(m * per * RB, (m + 1) * per * RB)
            high, low = yh[at_rows, :], yl[at_rows, :]
            main = s2t[:, 0:2 * ch]
            part = mm(high, main) + mm(low, main) + mm(high, s2t[:, 2 * ch:4 * ch])
            zp[it, m * per:(m + 1) * per] = part.reshape(per, RB, 2 * ch)
        posts = []
        for o, k in enumerate(far_first):
            for q in range(1, NX):
                i = slot()
                xx = plus(x, q, NX)
                pending.append(start(zp.at[it, at(plus(z, k, NZ), xx)], rx.at[it, q - 1, o], dev(at(z, xx), core, y), i))
                posts.append(i)
        return it, posts, []

    def normal_relay(state, o):
        it, posts, back = state
        k = far_first[o]
        for q in range(1, NX):
            arrived(rx.at[it, q - 1, o], posts[o * (NX - 1) + q - 1])
        total = zp[it, at(plus(z, k, NZ), x)]
        for q in range(1, NX):
            total = total + rx[it, q - 1, o]
        zs[it, o] = total
        if k:
            i = slot()
            pending.append(start(zs.at[it, o], rz.at[it, o], dev(at(plus(z, k, NZ), x), core, y), i))
            back.append((o, i))

    def normal_finish(state):
        it, _, back = state
        mine = zs[it, NZ - 1]
        for o, i in back:
            arrived(rz.at[it, o], i)
            mine = mine + rz[it, o]
        return mine

    def share(src, ref_of):
        posts = []
        for dy, dc in peers[::-1]:
            i = slot()
            yy, cc = plus(y, dy, NY), plus(core, dc, 2)
            pending.append(start(src, ref_of(b), dev(t, cc, yy), i))
            posts.append((plus(y, NY - dy, NY) * 2 + plus(core, dc, 2), i))
        return ref_of, posts

    def shared(state):
        ref_of, posts = state
        for bb, i in posts[::-1]:
            arrived(ref_of(bb), i)

    def rows_share(it, chunk):
        pz[it, b] = chunk
        return share(pz.at[it, b], lambda bb: pz.at[it, bb])

    def along_z(it, product):
        gz[it, z] = product
        posts = []
        for k in near_first(NZ)[::-1]:
            i = slot()
            pending.append(start(gz.at[it, z], gz.at[it, z], dev(at(plus(z, k, NZ), x), core, y), i))
            posts.append((plus(z, NZ - k, NZ), i))
        return it, posts

    def along_x(state):
        it, posts = state
        for zz, i in posts[::-1]:
            arrived(gz.at[it, zz], i)
        total = gz[it, 0]
        for k in range(1, NZ):
            total = total + gz[it, k]
        gx[it, x] = total
        posts = []
        for k in near_first(NX)[::-1]:
            i = slot()
            pending.append(start(gx.at[it, x], gx.at[it, x], dev(at(z, plus(x, k, NX)), core, y), i))
            posts.append((plus(x, NX - k, NX), i))
        return it, posts

    def gram_share(state):
        it, posts = state
        for xx, i in posts[::-1]:
            arrived(gx.at[it, xx], i)
        total = gx[it, 0]
        for k in range(1, NX):
            total = total + gx[it, k]
        gp[it, b] = total
        return share(gp.at[it, b], lambda bb: gp.at[it, bb])

    def factor_start(it):
        line = lax.broadcasted_iota(jnp.int32, (rank, rank), 0)
        column = lax.broadcasted_iota(jnp.int32, (rank, rank), 1)
        aug[:, :rank] = gp[it].reshape(rank, rank)
        aug[:, rank:] = jnp.where(line == column, 1.0, 0.0).astype(F32)

    def factor_panels(it, low, high):
        sub = lax.broadcasted_iota(jnp.int32, (PANEL, rank), 0)

        def panel(k, carry):
            top = pl.multiple_of(k * PANEL, PANEL)
            left = aug[pl.ds(top, PANEL), :rank]
            right = aug[pl.ds(top, PANEL), rank:]
            turned = pltpu.roll(left, lax.rem(rank - k * PANEL, rank), 1)
            cols = [jnp.broadcast_to(turned[:, q:q + 1], (PANEL, rank)) for q in range(PANEL)]
            done_left = jnp.zeros((PANEL, rank), F32)
            done_right = done_left

            def line(value, p):
                return jnp.broadcast_to(value[p:p + 1, :], (PANEL, rank))

            for p in range(PANEL):
                root = lax.rsqrt(line(cols[p], p))
                step = cols[p] * root
                for q in range(p + 1, PANEL):
                    cols[q] = cols[q] - step * (line(cols[q], p) * root)
                left_line = line(left, p) * root
                right_line = line(right, p) * root
                done_left = jnp.where(sub == p, left_line, done_left)
                done_right = jnp.where(sub == p, right_line, done_right)
                left = left - step * left_line
                right = right - step * right_line
            both = jnp.concatenate([done_left, done_right], axis=1)
            fac[it, pl.ds(top, PANEL), :] = done_right
            aug[...] = aug[...] - exact(done_left, both, ((0,), (0,)))
            return carry

        lax.fori_loop(low, high, panel, 0)

    panels = rank // PANEL
    order = near_first(NZ)
    moving = gather_start(0, first_chunk)
    gather_relay(moving, order)
    setup_tile()
    gather_finish(moving)
    folding = normal_start(0, analyse(0))
    for o in range(NZ):
        normal_relay(folding, o)
    chunk = normal_finish(folding)

    moving = gather_start(1, chunk)
    joined = rows_share(0, chunk)
    gather_relay(moving, order[:2])
    shared(joined)
    gram = along_z(0, exact(pz[0, b], pz[0].reshape(rank, 2 * ch), ((1,), (1,))))
    gather_relay(moving, order[2:])
    early = (NX - 1) * (NZ // 2)
    gather_finish(moving, 0, early)
    gram = along_x(gram)
    gather_finish(moving, early)
    image = analyse(1)
    folding = normal_start(1, image)
    gram = gram_share(gram)
    head = max(NZ - 5, 1)
    for o in range(head):
        normal_relay(folding, o)
    shared(gram)
    factor_start(0)
    for o in range(head, NZ):
        factor_panels(0, o - head, o - head + 1)
        normal_relay(folding, o)
    factor_panels(0, NZ - head, panels)
    chunk = normal_finish(folding)
    joined = rows_share(1, chunk)
    shared(joined)
    vfull[...] = exact(fac[0], pz[1].reshape(rank, 2 * ch)).reshape(blocks, RB, 2 * ch)

    chunk = vfull[b]
    gram = along_z(1, exact(chunk, vfull[...].reshape(rank, 2 * ch), ((1,), (1,))))
    moving = gather_start(2, chunk)
    gather_relay(moving, order[:4])
    gram = along_x(gram)
    gather_relay(moving, order[4:])
    gram = gram_share(gram)
    gather_finish(moving)
    yx[b] = analyse(2)[:, :width - PAD]
    joined = share(yx.at[b], lambda bb: yx.at[bb])
    turned_high, turned_low = split(vall[2].reshape(tiles * RB, 2 * ch).T)
    shared(gram)
    factor_start(1)
    factor_panels(1, 0, panels)
    inverse = fac[1]
    fac[0] = inverse.T
    both = exact(inverse, vfull[...].reshape(rank, 2 * ch))
    aug[:, :rank] = jnp.where(core == 0, both[:, :ch], both[:, ch:]).T
    bout_ref[...] = aug[pl.ds(pl.multiple_of(y * CHG, CHG), CHG), :rank]
    weights = exact(fac[0, pl.ds(pl.multiple_of(b * RB, RB), RB), :], inverse)
    shared(joined)
    image = exact(weights, yx[...].reshape(rank, width - PAD))
    spread(jnp.concatenate([image, jnp.zeros((RB, PAD), F32)], axis=1))
    for bit in range(2):
        at_rows = slice(bit * ch, (bit + 1) * ch)
        part = (
            mm(turned_high[at_rows], yh[...])
            + mm(turned_low[at_rows], yh[...])
            + mm(turned_high[at_rows], yl[...])
        )
        if bit:
            total = total + pltpu.roll(part, 1, 1)
        else:
            total = part
    for half in range(2):
        piece = total[:, PAD + half * HALF:PAD + (half + 1) * HALF]
        ep[half] = piece.reshape(NY, CHG, HALF)
    other = 1 - core
    order = near_first(NY)[::-1] + [0]
    posts = []
    for dy in order:
        i = slot()
        yy = plus(y, dy, NY)
        pending.append(start(ep.at[other, yy], er.at[yy], dev(t, other, y), i))
        posts.append(i)
    back = []
    for dy, i in zip(order, posts):
        yy = plus(y, dy, NY)
        arrived(er.at[yy], i)
        piece = ep[core, yy] + er[yy]
        if dy:
            es[dy] = piece
            j = slot()
            pending.append(start(es.at[dy], ey.at[dy], dev(t, core, yy), j))
            back.append((dy, j))
        else:
            estimate = piece
    for dy, j in back:
        arrived(ey.at[dy], j)
        estimate = estimate + ey[dy]
    estimate = estimate * (1.0 / (2 * tiles))
    residual = mask_ref[...].astype(F32) * (ks_ref[...] - estimate)
    rec_ref[...] = estimate + residual - jnp.clip(residual, -THRESHOLD, THRESHOLD)
    for copy in pending + waiting:
        copy.wait_send()
    assert used[0] <= SEMS, used[0]


def shards(kspace, sample_mask, start_basis):
    tiles = NZ * NX
    ch = NY * CHG
    width = 2 * HALF + 2 * PAD
    blocks = 2 * NY
    rank = blocks * RB
    vmem = pltpu.VMEM
    recovered, basis = pl.pallas_call(
        kernel,
        out_shape=(
            jax.ShapeDtypeStruct((CHG, HALF), F32),
            jax.ShapeDtypeStruct((CHG, rank), F32),
        ),
        in_specs=[pl.BlockSpec(memory_space=pl.ANY)] * 3,
        out_specs=(pl.BlockSpec(memory_space=pltpu.VMEM),) * 2,
        scratch_shapes=[
            vmem((CHG, HALF), F32),
            vmem((CHG, HALF), jnp.int32),
            vmem((CHG, rank), F32),
            vmem((CHG, HALF), F32),
            vmem((2, NY, CHG, HALF), F32),
            vmem((CHG, PAD), F32),
            vmem((2, NY, CHG, PAD), F32),
            vmem((blocks, RB, ch), F32),
            vmem((2, NY, RB, ch), F32),
            vmem((ITERS + 1, tiles, RB, 2 * ch), F32),
            vmem((6 * ch, width), BF16),
            vmem((width, 4 * ch), BF16),
            vmem((tiles * RB, width), F32),
            vmem((tiles * RB, width), BF16),
            vmem((tiles * RB, width), BF16),
            vmem((ITERS, tiles, RB, 2 * ch), F32),
            vmem((ITERS, max(NX - 1, 1), NZ, RB, 2 * ch), F32),
            vmem((ITERS, NZ, RB, 2 * ch), F32),
            vmem((ITERS, NZ, RB, 2 * ch), F32),
            vmem((ITERS, blocks, RB, 2 * ch), F32),
            vmem((ITERS, NZ, RB, rank), F32),
            vmem((ITERS, NX, RB, rank), F32),
            vmem((ITERS, blocks, RB, rank), F32),
            vmem((rank, 2 * rank), F32),
            vmem((ITERS, rank, rank), F32),
            vmem((blocks, RB, 2 * ch), F32),
            vmem((blocks, RB, width - PAD), F32),
            vmem((2, NY, CHG, HALF), F32),
            vmem((NY, CHG, HALF), F32),
            vmem((NY, CHG, HALF), F32),
            vmem((NY, CHG, HALF), F32),
            pltpu.SemaphoreType.DMA((SEMS,)),
            pltpu.SemaphoreType.DMA((SEMS,)),
            pltpu.SemaphoreType.DMA((3,)),
        ],
        compiler_params=pltpu.CompilerParams(
            collective_id=0, has_side_effects=True, vmem_limit_bytes=48 << 20
        ),
    )(kspace, sample_mask, start_basis.reshape(CHG, rank))
    return recovered, basis.reshape(1, CHG, rank)


def solution(mesh):
    return jax.shard_map(
        shards,
        mesh=mesh,
        in_specs=(P("coil", "rows"), P("coil", "rows"), P("coil", "rows", None)),
        out_specs=(P("coil", "rows"), P("coil", "rows", None)),
        check_vma=False,
    )
```

```python
import functools

import jax
import jax.numpy as jnp
from jax import lax
from jax.experimental import pallas as pl
from jax.experimental.pallas import tpu as pltpu
from jax.sharding import PartitionSpec as P

NZ, NX, NY = 8, 4, 4
ITERS = 2
CHG = 32
HALF = 512
RB = 16
THRESHOLD = 0.05
MESH = pl.DeviceIdType.MESH
HIGHEST = lax.Precision.HIGHEST
F32 = jnp.float32
BF16 = jnp.bfloat16
PAD = 128
PANEL = 16
SEMS = 256


def split(value):
    high = value.astype(BF16)
    return high, (value - high.astype(F32)).astype(BF16)


def mm(a, b, dims=((1,), (0,))):
    return lax.dot_general(a, b, (dims, ((), ())), preferred_element_type=F32)


def exact(a, b, dims=((1,), (0,))):
    return lax.dot_general(
        a, b, (dims, ((), ())), precision=HIGHEST, preferred_element_type=F32
    )


def near_first(n):
    return sorted(range(1, n), key=lambda k: min(k, n - k))


def kernel(
    ks_hbm, mask_hbm, basis_hbm, rec_ref, bout_ref,
    ks_ref, mask_ref, basis_ref, own, sb, edge, halo, bt, vx, vall, s3, s2t, ubuf, yh, yl,
    zp, rx, zs, rz, pz, gz, gx, gp, aug, fac, vfull, yx, ep, er, es, ey,
    send, recv, load,
):
    loads = [
        pltpu.make_async_copy(src, dst, load.at[i])
        for i, (src, dst) in enumerate(
            ((basis_hbm, basis_ref), (ks_hbm, ks_ref), (mask_hbm, mask_ref))
        )
    ]
    for copy in loads:
        copy.start()
    tiles = NZ * NX
    ch = NY * CHG
    width = 2 * HALF + 2 * PAD
    blocks = 2 * NY
    rank = blocks * RB
    rows = lax.axis_index("rows")
    y = lax.axis_index("coil")
    core = lax.rem(rows, 2)
    t = lax.div(rows, 2)
    x = lax.rem(t, NX)
    z = lax.div(t, NX)
    b = y * 2 + core
    used = [0]

    def dev(tile, c, yy):
        return (tile * 2 + c, yy)

    def slot():
        used[0] += 1
        return used[0] - 1

    def start(src, dst, device, i, j=None):
        copy = pltpu.make_async_remote_copy(
            src_ref=src, dst_ref=dst, send_sem=send.at[i],
            recv_sem=recv.at[i if j is None else j],
            device_id=device, device_id_type=MESH,
        )
        copy.start()
        return copy

    def arrived(dst, i):
        pltpu.make_async_remote_copy(
            src_ref=dst, dst_ref=dst, send_sem=send.at[i], recv_sem=recv.at[i],
            device_id=(rows, y), device_id_type=MESH,
        ).wait_recv()

    def at(zz, xx):
        return zz * NX + xx

    def plus(v, k, n):
        return lax.rem(v + k, n)

    ring = [(dy, dc) for dy in (0, 1, 3, 2) if dy < NY for dc in range(2)]
    peers = [p for p in ring if p != (0, 0)]
    before, after = plus(t, tiles - 1, tiles), plus(t, 1, tiles)

    barrier = pltpu.get_barrier_semaphore()
    greeted = 0
    for k in range(1, NZ):
        pl.semaphore_signal(barrier, inc=1, device_id=dev(at(plus(z, k, NZ), x), core, y), device_id_type=MESH)
        greeted += 1
    for k in range(1, NX):
        pl.semaphore_signal(barrier, inc=1, device_id=dev(at(z, plus(x, k, NX)), core, y), device_id_type=MESH)
        greeted += 1
    for dy, dc in peers:
        pl.semaphore_signal(barrier, inc=1, device_id=dev(t, plus(core, dc, 2), plus(y, dy, NY)), device_id_type=MESH)
        greeted += 1
    for tile in (before, after):
        for dy, dc in ring:
            pl.semaphore_signal(barrier, inc=1, device_id=dev(tile, plus(core, dc, 2), plus(y, dy, NY)), device_id_type=MESH)
            greeted += 1
    for copy in loads:
        copy.wait()
    lanes = lax.broadcasted_iota(jnp.int32, (rank, ch), 1)
    tiled = jnp.concatenate([basis_ref[...]] * NY, axis=0).T
    placed = jnp.where(lax.div(lanes, CHG) == y, tiled, 0.0)
    bt[...] = placed.reshape(blocks, RB, ch)
    sampled = ks_ref[...] * mask_ref[...].astype(F32)
    own[...] = sampled
    edge[...] = jnp.where(core == 0, sampled[:, :PAD], sampled[:, HALF - PAD:])
    pl.semaphore_wait(barrier, greeted)

    waiting = []
    basis_in = []
    for dy, dc in peers:
        i = slot()
        yy, cc = plus(y, dy, NY), plus(core, dc, 2)
        waiting.append(start(bt.at[yy * 2 + cc], vx.at[core, y], dev(t, cc, yy), i))
        basis_in.append((plus(core, dc, 2), plus(y, NY - dy, NY), i))
    tile_in = []
    for dy, dc in peers:
        i = slot()
        yy, cc = plus(y, dy, NY), plus(core, dc, 2)
        waiting.append(start(own, sb.at[core, y], dev(t, cc, yy), i))
        tile_in.append((plus(core, dc, 2), plus(y, NY - dy, NY), i))
    halo_base = [slot() for _ in range(2 * NY)]
    target = lax.rem(t + tiles + 2 * core - 1, tiles)
    for dy, dc in ring:
        i = halo_base[dc * NY + dy]
        yy, cc = plus(y, dy, NY), plus(core, dc, 2)
        waiting.append(start(edge, halo.at[core, y], dev(target, cc, yy), i, halo_base[0] + core * NY + dy))
    vx[core, y] = bt[b]
    sb[core, y] = own[...]
    for cc, yy, i in basis_in:
        arrived(vx.at[cc, yy], i)
    halves = []
    for half in range(2):
        total = vx[half, 0]
        for yy in range(1, NY):
            total = total + vx[half, yy]
        halves.append(total)
    first_chunk = jnp.concatenate(halves, axis=1)

    pending = []

    def gather_start(it, chunk):
        vall[it, t] = chunk
        first = {}
        for k in near_first(NZ):
            first[k] = slot()
            pending.append(start(vall.at[it, t], vall.at[it, t], dev(at(plus(z, k, NZ), x), core, y), first[k]))
        second = []
        gather_relay((it, first, second), (0,))
        return it, first, second

    def gather_relay(state, steps):
        it, first, second = state
        for k in steps:
            zz = plus(z, NZ - k, NZ)
            here = at(zz, x)
            if k:
                arrived(vall.at[it, here], first[k])
            for q in range(1, NX):
                i = slot()
                pending.append(start(vall.at[it, here], vall.at[it, here], dev(at(z, plus(x, q, NX)), core, y), i))
                second.append((at(zz, plus(x, NX - q, NX)), i))

    def gather_multiply(state, pairs):
        it, _, second = state
        slabs = [0] + near_first(NZ)
        for u in pairs:
            for here, i in second[2 * u * (NX - 1):2 * (u + 1) * (NX - 1)]:
                arrived(vall.at[it, here], i)
            parts, places = [], []
            for k in slabs[2 * u:2 * u + 2]:
                zz = plus(z, NZ - k, NZ)
                parts.append(vall[it, pl.ds(zz * NX, NX)].reshape(NX * RB, 2 * ch))
                places.append(pl.multiple_of(zz * NX * RB, NX * RB))
            high, low = split(jnp.concatenate(parts, axis=0))
            product = mm(jnp.concatenate([high, high, low], axis=1), s3[...])
            for w, place in enumerate(places):
                ubuf[pl.ds(place, NX * RB), :] = product[w * NX * RB:(w + 1) * NX * RB]

    def analyse():
        image = ubuf[0:RB, :]
        for i in range(1, tiles):
            image = image + pltpu.roll(ubuf[i * RB:(i + 1) * RB, :], width - 2 * i, 1)
        return image

    def spread(image):
        for i in range(tiles):
            moved = image if i == 0 else pltpu.roll(image, 2 * i, 1)
            high, low = split(moved)
            yh[i * RB:(i + 1) * RB, :] = high
            yl[i * RB:(i + 1) * RB, :] = low

    def setup_tile():
        for cc, yy, i in tile_in:
            arrived(sb.at[cc, yy], i)
        for s in range(2):
            for dy in range(NY):
                arrived(halo.at[s, plus(y, NY - dy, NY)], halo_base[s * NY + dy])
        full = jnp.concatenate(
            [
                jnp.concatenate([halo[1, g], sb[0, g], sb[1, g], halo[0, g]], axis=1)
                for g in range(NY)
            ],
            axis=0,
        )
        pair = jnp.concatenate([full, pltpu.roll(full, width - 1, 1)], axis=0)
        high, low = split(pair)
        s3[0:2 * ch, :] = high
        s3[2 * ch:4 * ch, :] = low
        s3[4 * ch:6 * ch, :] = high
        turned_high, turned_low = split(pair.T)
        s2t[:, 0:2 * ch] = turned_high
        s2t[:, 2 * ch:4 * ch] = turned_low

    couples = NZ // 2
    far_first = near_first(couples)[::-1] + [0]

    def normal_start(it, image, hook=None):
        place = lax.broadcasted_iota(jnp.int32, (RB, width), 1)
        spread(jnp.where(jnp.logical_and(place >= PAD, place < PAD + 2 * HALF), image, 0.0))
        half, odd = lax.div(z, 2), lax.rem(z, 2)
        steps = []
        for g in far_first:
            pair = plus(half, g, couples)
            size = 2 * NX * RB
            at_rows = pl.ds(pl.multiple_of(pair * size, size), size)
            high, low = yh[at_rows, :], yl[at_rows, :]
            main = s2t[:, 0:2 * ch]
            part = mm(high, main) + mm(low, main) + mm(high, s2t[:, 2 * ch:4 * ch])
            zp[it, pl.ds(pair * 2 * NX, 2 * NX)] = part.reshape(2 * NX, RB, 2 * ch)
            for w in range(2):
                o = len(steps)
                zz = 2 * pair + w if g else 2 * half + (odd if w else 1 - odd)
                posts = []
                for q in range(1, NX):
                    i = slot()
                    xx = plus(x, q, NX)
                    pending.append(start(zp.at[it, at(zz, xx)], rx.at[it, q - 1, o], dev(at(z, xx), core, y), i))
                    posts.append(i)
                steps.append((zz, posts))
            if hook is not None and len(steps) == min(4, NZ):
                hook()
        return it, steps, [slot() for _ in range(NZ)]

    def normal_relay(state, o):
        it, steps, back = state
        zz, posts = steps[o]
        for q in range(1, NX):
            arrived(rx.at[it, q - 1, o], posts[q - 1])
        total = zp[it, at(zz, x)]
        for q in range(1, NX):
            total = total + rx[it, q - 1, o]
        zs[it, o] = total
        if o < NZ - 1:
            away = lax.rem(zz - z + NZ, NZ)
            pending.append(start(zs.at[it, o], rz.at[it, z], dev(at(zz, x), core, y), back[o], back[0] + away))

    def normal_finish(state):
        it, _, back = state
        mine = zs[it, NZ - 1]
        for k in range(1, NZ):
            source = plus(z, NZ - k, NZ)
            arrived(rz.at[it, source], back[0] + k)
            mine = mine + rz[it, source]
        return mine

    def share(src, ref_of):
        posts = []
        for dy, dc in peers[::-1]:
            i = slot()
            yy, cc = plus(y, dy, NY), plus(core, dc, 2)
            pending.append(start(src, ref_of(b), dev(t, cc, yy), i))
            posts.append((plus(y, NY - dy, NY) * 2 + plus(core, dc, 2), i))
        return ref_of, posts

    def shared(state):
        ref_of, posts = state
        for bb, i in posts[::-1]:
            arrived(ref_of(bb), i)

    def rows_share(it, chunk):
        pz[it, b] = chunk
        return share(pz.at[it, b], lambda bb: pz.at[it, bb])

    def along_z(it, product):
        gz[it, z] = product
        posts = []
        for k in near_first(NZ)[::-1]:
            i = slot()
            pending.append(start(gz.at[it, z], gz.at[it, z], dev(at(plus(z, k, NZ), x), core, y), i))
            posts.append((plus(z, NZ - k, NZ), i))
        return it, posts

    def along_x(state):
        it, posts = state
        for zz, i in posts[::-1]:
            arrived(gz.at[it, zz], i)
        total = gz[it, 0]
        for k in range(1, NZ):
            total = total + gz[it, k]
        gx[it, x] = total
        posts = []
        for k in near_first(NX)[::-1]:
            i = slot()
            pending.append(start(gx.at[it, x], gx.at[it, x], dev(at(z, plus(x, k, NX)), core, y), i))
            posts.append((plus(x, NX - k, NX), i))
        return it, posts

    def gram_share(state):
        it, posts = state
        for xx, i in posts[::-1]:
            arrived(gx.at[it, xx], i)
        total = gx[it, 0]
        for k in range(1, NX):
            total = total + gx[it, k]
        gp[it, b] = total
        return share(gp.at[it, b], lambda bb: gp.at[it, bb])

    def factor_start(it):
        line = lax.broadcasted_iota(jnp.int32, (rank, rank), 0)
        column = lax.broadcasted_iota(jnp.int32, (rank, rank), 1)
        aug[:, :rank] = gp[it].reshape(rank, rank)
        aug[:, rank:] = jnp.where(line == column, 1.0, 0.0).astype(F32)

    def factor_panels(it, low, high):
        sub = lax.broadcasted_iota(jnp.int32, (PANEL, rank), 0)

        def panel(k, carry):
            top = pl.multiple_of(k * PANEL, PANEL)
            left = aug[pl.ds(top, PANEL), :rank]
            right = aug[pl.ds(top, PANEL), rank:]
            turned = pltpu.roll(left, lax.rem(rank - k * PANEL, rank), 1)
            cols = [jnp.broadcast_to(turned[:, q:q + 1], (PANEL, rank)) for q in range(PANEL)]
            done_left = jnp.zeros((PANEL, rank), F32)
            done_right = done_left

            def line(value, p):
                return jnp.broadcast_to(value[p:p + 1, :], (PANEL, rank))

            for p in range(PANEL):
                root = lax.rsqrt(line(cols[p], p))
                step = cols[p] * root
                for q in range(p + 1, PANEL):
                    cols[q] = cols[q] - step * (line(cols[q], p) * root)
                left_line = line(left, p) * root
                right_line = line(right, p) * root
                done_left = jnp.where(sub == p, left_line, done_left)
                done_right = jnp.where(sub == p, right_line, done_right)
                left = left - step * left_line
                right = right - step * right_line
            both = jnp.concatenate([done_left, done_right], axis=1)
            fac[it, pl.ds(top, PANEL), :] = done_right
            aug[...] = aug[...] - exact(done_left, both, ((0,), (0,)))
            return carry

        lax.fori_loop(low, high, panel, 0)

    panels = rank // PANEL
    order = near_first(NZ)
    moving = gather_start(0, first_chunk)
    gather_relay(moving, order)
    setup_tile()
    every = range(couples)
    gather_multiply(moving, every)
    folding = normal_start(0, analyse())
    for o in range(NZ):
        normal_relay(folding, o)
    chunk = normal_finish(folding)

    moving = gather_start(1, chunk)
    joined = rows_share(0, chunk)
    gather_relay(moving, order[:2])
    shared(joined)
    gram = along_z(0, exact(pz[0, b], pz[0].reshape(rank, 2 * ch), ((1,), (1,))))
    gather_relay(moving, order[2:])
    gather_multiply(moving, every[:couples // 2])
    gram = along_x(gram)
    gather_multiply(moving, every[couples // 2:])
    grams = []
    folding = normal_start(1, analyse(), lambda: grams.append(gram_share(gram)))
    gram = grams[0]
    head = max(NZ - 5, 1)
    for o in range(head):
        normal_relay(folding, o)
    shared(gram)
    factor_start(0)
    for o in range(head, NZ):
        factor_panels(0, o - head, o - head + 1)
        normal_relay(folding, o)
    factor_panels(0, NZ - head, panels)
    chunk = normal_finish(folding)
    joined = rows_share(1, chunk)
    shared(joined)
    vfull[...] = exact(fac[0], pz[1].reshape(rank, 2 * ch)).reshape(blocks, RB, 2 * ch)

    chunk = vfull[b]
    gram = along_z(1, exact(chunk, vfull[...].reshape(rank, 2 * ch), ((1,), (1,))))
    moving = gather_start(2, chunk)
    gather_relay(moving, order[:4])
    gram = along_x(gram)
    gather_relay(moving, order[4:])
    gram = gram_share(gram)
    gather_multiply(moving, every)
    yx[b] = analyse()[:, :width - PAD]
    joined = share(yx.at[b], lambda bb: yx.at[bb])
    turned_high, turned_low = split(vall[2].reshape(tiles * RB, 2 * ch).T)
    shared(gram)
    factor_start(1)
    factor_panels(1, 0, panels)
    inverse = fac[1]
    fac[0] = inverse.T
    weights = exact(fac[0, pl.ds(pl.multiple_of(b * RB, RB), RB), :], inverse)
    shared(joined)
    image = exact(weights, yx[...].reshape(rank, width - PAD))
    spread(jnp.concatenate([image, jnp.zeros((RB, PAD), F32)], axis=1))
    for bit in range(2):
        at_rows = slice(bit * ch, (bit + 1) * ch)
        part = (
            mm(turned_high[at_rows], yh[...])
            + mm(turned_low[at_rows], yh[...])
            + mm(turned_high[at_rows], yl[...])
        )
        if bit:
            total = total + pltpu.roll(part, 1, 1)
        else:
            total = part
    for half in range(2):
        piece = total[:, PAD + half * HALF:PAD + (half + 1) * HALF]
        ep[half] = piece.reshape(NY, CHG, HALF)
    other = 1 - core
    order = near_first(NY)[::-1] + [0]
    posts = []
    for dy in order:
        i = slot()
        yy = plus(y, dy, NY)
        pending.append(start(ep.at[other, yy], er.at[yy], dev(t, other, y), i))
        posts.append(i)
    back = []
    for dy, i in zip(order, posts):
        yy = plus(y, dy, NY)
        arrived(er.at[yy], i)
        piece = ep[core, yy] + er[yy]
        if dy:
            es[dy] = piece
            j = slot()
            pending.append(start(es.at[dy], ey.at[dy], dev(t, core, yy), j))
            back.append((dy, j))
        else:
            estimate = piece
    both = exact(inverse, vfull[...].reshape(rank, 2 * ch))
    aug[:, :rank] = jnp.where(core == 0, both[:, :ch], both[:, ch:]).T
    bout_ref[...] = aug[pl.ds(pl.multiple_of(y * CHG, CHG), CHG), :rank]
    for dy, j in back:
        arrived(ey.at[dy], j)
        estimate = estimate + ey[dy]
    estimate = estimate * (1.0 / (2 * tiles))
    residual = mask_ref[...].astype(F32) * (ks_ref[...] - estimate)
    rec_ref[...] = estimate + residual - jnp.clip(residual, -THRESHOLD, THRESHOLD)
    for copy in pending + waiting:
        copy.wait_send()
    assert used[0] <= SEMS, used[0]


def shards(kspace, sample_mask, start_basis):
    tiles = NZ * NX
    ch = NY * CHG
    width = 2 * HALF + 2 * PAD
    blocks = 2 * NY
    rank = blocks * RB
    vmem = pltpu.VMEM
    recovered, basis = pl.pallas_call(
        kernel,
        out_shape=(
            jax.ShapeDtypeStruct((CHG, HALF), F32),
            jax.ShapeDtypeStruct((CHG, rank), F32),
        ),
        in_specs=[pl.BlockSpec(memory_space=pltpu.HBM)] * 3,
        out_specs=(pl.BlockSpec(memory_space=pltpu.VMEM),) * 2,
        scratch_shapes=[
            vmem((CHG, HALF), F32),
            vmem((CHG, HALF), jnp.int32),
            vmem((CHG, rank), F32),
            vmem((CHG, HALF), F32),
            vmem((2, NY, CHG, HALF), F32),
            vmem((CHG, PAD), F32),
            vmem((2, NY, CHG, PAD), F32),
            vmem((blocks, RB, ch), F32),
            vmem((2, NY, RB, ch), F32),
            vmem((ITERS + 1, tiles, RB, 2 * ch), F32),
            vmem((6 * ch, width), BF16),
            vmem((width, 4 * ch), BF16),
            vmem((tiles * RB, width), F32),
            vmem((tiles * RB, width), BF16),
            vmem((tiles * RB, width), BF16),
            vmem((ITERS, tiles, RB, 2 * ch), F32),
            vmem((ITERS, max(NX - 1, 1), NZ, RB, 2 * ch), F32),
            vmem((ITERS, NZ, RB, 2 * ch), F32),
            vmem((ITERS, NZ, RB, 2 * ch), F32),
            vmem((ITERS, blocks, RB, 2 * ch), F32),
            vmem((ITERS, NZ, RB, rank), F32),
            vmem((ITERS, NX, RB, rank), F32),
            vmem((ITERS, blocks, RB, rank), F32),
            vmem((rank, 2 * rank), F32),
            vmem((ITERS, rank, rank), F32),
            vmem((blocks, RB, 2 * ch), F32),
            vmem((blocks, RB, width - PAD), F32),
            vmem((2, NY, CHG, HALF), F32),
            vmem((NY, CHG, HALF), F32),
            vmem((NY, CHG, HALF), F32),
            vmem((NY, CHG, HALF), F32),
            pltpu.SemaphoreType.DMA((SEMS,)),
            pltpu.SemaphoreType.DMA((SEMS,)),
            pltpu.SemaphoreType.DMA((3,)),
        ],
        compiler_params=pltpu.CompilerParams(
            collective_id=0, has_side_effects=True, vmem_limit_bytes=67043328
        ),
    )(kspace, sample_mask, start_basis.reshape(CHG, rank))
    return recovered, basis.reshape(1, CHG, rank)


def solution(mesh):
    return jax.shard_map(
        shards,
        mesh=mesh,
        in_specs=(P("coil", "rows"), P("coil", "rows"), P("coil", "rows", None)),
        out_specs=(P("coil", "rows"), P("coil", "rows", None)),
        check_vma=False,
    )
```

```python
import functools

import jax
import jax.numpy as jnp
from jax import lax
from jax.experimental import pallas as pl
from jax.experimental.pallas import tpu as pltpu
from jax.sharding import PartitionSpec as P

NZ, NX, NY = 8, 4, 4
ITERS = 2
CHG = 32
HALF = 512
RB = 16
THRESHOLD = 0.05
MESH = pl.DeviceIdType.MESH
HIGHEST = lax.Precision.HIGHEST
F32 = jnp.float32
BF16 = jnp.bfloat16
PAD = 128
PANEL = 16
SEMS = 256


def split(value):
    high = value.astype(BF16)
    return high, (value - high.astype(F32)).astype(BF16)


def mm(a, b, dims=((1,), (0,))):
    return lax.dot_general(a, b, (dims, ((), ())), preferred_element_type=F32)


def exact(a, b, dims=((1,), (0,))):
    return lax.dot_general(
        a, b, (dims, ((), ())), precision=HIGHEST, preferred_element_type=F32
    )


def near_first(n):
    return sorted(range(1, n), key=lambda k: min(k, n - k))


def kernel(
    ks_hbm, mask_hbm, basis_hbm, rec_ref, bout_ref,
    ks_ref, mask_ref, basis_ref, own, sb, edge, halo, bt, vx, vall, s8h, s8l, s8th, s8tl, turned, yh, yl,
    zp, rx, zs, rz, pz, gz, gx, gp, aug, fac, vfull, ys, yx, es, ey,
    send, recv, load,
):
    loads = [
        pltpu.make_async_copy(src, dst, load.at[i])
        for i, (src, dst) in enumerate(
            ((basis_hbm, basis_ref), (ks_hbm, ks_ref), (mask_hbm, mask_ref))
        )
    ]
    for copy in loads:
        copy.start()
    tiles = NZ * NX
    ch = NY * CHG
    width = 2 * HALF + 2 * PAD
    span = HALF + PAD
    blocks = 2 * NY
    rank = blocks * RB
    rows = lax.axis_index("rows")
    y = lax.axis_index("coil")
    core = lax.rem(rows, 2)
    t = lax.div(rows, 2)
    x = lax.rem(t, NX)
    z = lax.div(t, NX)
    b = y * 2 + core
    used = [0]

    def dev(tile, c, yy):
        return (tile * 2 + c, yy)

    def slot():
        used[0] += 1
        return used[0] - 1

    def start(src, dst, device, i, j=None):
        copy = pltpu.make_async_remote_copy(
            src_ref=src, dst_ref=dst, send_sem=send.at[i],
            recv_sem=recv.at[i if j is None else j],
            device_id=device, device_id_type=MESH,
        )
        copy.start()
        return copy

    def arrived(dst, i):
        pltpu.make_async_remote_copy(
            src_ref=dst, dst_ref=dst, send_sem=send.at[i], recv_sem=recv.at[i],
            device_id=(rows, y), device_id_type=MESH,
        ).wait_recv()

    def at(zz, xx):
        return zz * NX + xx

    def plus(v, k, n):
        return lax.rem(v + k, n)

    ring = [(dy, dc) for dy in (0, 1, 3, 2) if dy < NY for dc in range(2)]
    peers = [p for p in ring if p != (0, 0)]
    before, after = plus(t, tiles - 1, tiles), plus(t, 1, tiles)

    barrier = pltpu.get_barrier_semaphore()
    greeted = 0
    for k in range(1, NZ):
        pl.semaphore_signal(barrier, inc=1, device_id=dev(at(plus(z, k, NZ), x), core, y), device_id_type=MESH)
        greeted += 1
    for k in range(1, NX):
        pl.semaphore_signal(barrier, inc=1, device_id=dev(at(z, plus(x, k, NX)), core, y), device_id_type=MESH)
        greeted += 1
    for dy, dc in peers:
        pl.semaphore_signal(barrier, inc=1, device_id=dev(t, plus(core, dc, 2), plus(y, dy, NY)), device_id_type=MESH)
        greeted += 1
    for tile in (before, after):
        for dy, dc in ring:
            pl.semaphore_signal(barrier, inc=1, device_id=dev(tile, plus(core, dc, 2), plus(y, dy, NY)), device_id_type=MESH)
            greeted += 1
    for copy in loads:
        copy.wait()
    lanes = lax.broadcasted_iota(jnp.int32, (rank, ch), 1)
    tiled = jnp.concatenate([basis_ref[...]] * NY, axis=0).T
    placed = jnp.where(lax.div(lanes, CHG) == y, tiled, 0.0)
    bt[...] = placed.reshape(blocks, RB, ch)
    sampled = ks_ref[...] * mask_ref[...].astype(F32)
    own[...] = sampled
    edge[...] = jnp.where(core == 0, sampled[:, :PAD], sampled[:, HALF - PAD:])
    pl.semaphore_wait(barrier, greeted)

    waiting = []
    basis_in = []
    for dy, dc in peers:
        i = slot()
        yy, cc = plus(y, dy, NY), plus(core, dc, 2)
        waiting.append(start(bt.at[yy * 2 + cc], vx.at[core, y], dev(t, cc, yy), i))
        basis_in.append((plus(core, dc, 2), plus(y, NY - dy, NY), i))
    tile_in = []
    for dy, dc in peers:
        i = slot()
        yy, cc = plus(y, dy, NY), plus(core, dc, 2)
        waiting.append(start(own, sb.at[core, y], dev(t, cc, yy), i))
        tile_in.append((plus(core, dc, 2), plus(y, NY - dy, NY), i))
    halo_base = [slot() for _ in range(2 * NY)]
    target = lax.rem(t + tiles + 2 * core - 1, tiles)
    for dy, dc in ring:
        i = halo_base[dc * NY + dy]
        yy, cc = plus(y, dy, NY), plus(core, dc, 2)
        waiting.append(start(edge, halo.at[core, y], dev(target, cc, yy), i, halo_base[0] + core * NY + dy))
    vx[core, y] = bt[b]
    sb[core, y] = own[...]
    for cc, yy, i in basis_in:
        arrived(vx.at[cc, yy], i)
    halves = []
    for half in range(2):
        total = vx[half, 0]
        for yy in range(1, NY):
            total = total + vx[half, yy]
        halves.append(total)
    first_chunk = jnp.concatenate(halves, axis=1)

    pending = []

    def gather_start(it, chunk):
        vall[it, t] = chunk
        first = {}
        for k in near_first(NZ):
            first[k] = slot()
            pending.append(start(vall.at[it, t], vall.at[it, t], dev(at(plus(z, k, NZ), x), core, y), first[k]))
        second = []
        gather_relay((it, first, second), (0,))
        return it, first, second

    def gather_relay(state, steps):
        it, first, second = state
        for k in steps:
            zz = plus(z, NZ - k, NZ)
            here = at(zz, x)
            if k:
                arrived(vall.at[it, here], first[k])
            for q in range(1, NX):
                i = slot()
                pending.append(start(vall.at[it, here], vall.at[it, here], dev(at(z, plus(x, q, NX)), core, y), i))
                second.append((at(zz, plus(x, NX - q, NX)), i))

    def gather_finish(state, low=0, high=None):
        for here, i in state[2][low:high]:
            arrived(vall.at[state[0], here], i)

    def analyse(it):
        slabs = vall[it].reshape(NZ, NX, RB, 2 * ch)
        joined = jnp.concatenate(
            [slabs[:, q].reshape(NZ * RB, 2 * ch) for q in range(NX)], axis=1
        )
        high, low = split(joined)
        product = mm(high, s8h[...]) + mm(high, s8l[...]) + mm(low, s8h[...])
        image = product[0:RB]
        for k in range(1, NZ):
            image = image + pltpu.roll(product[k * RB:(k + 1) * RB], width - 2 * NX * k, 1)
        return image

    def setup_tile():
        for cc, yy, i in tile_in:
            arrived(sb.at[cc, yy], i)
        for s in range(2):
            for dy in range(NY):
                arrived(halo.at[s, plus(y, NY - dy, NY)], halo_base[s * NY + dy])
        full = jnp.concatenate(
            [
                jnp.concatenate([halo[1, g], sb[0, g], sb[1, g], halo[0, g]], axis=1)
                for g in range(NY)
            ],
            axis=0,
        )
        for shift in range(2 * NX):
            moved = full if shift == 0 else pltpu.roll(full, width - shift, 1)
            high, low = split(moved)
            s8h[shift * ch:(shift + 1) * ch, :] = high
            s8l[shift * ch:(shift + 1) * ch, :] = low
        turned[0:width, :] = full.T
        turned[width:width + 8, :] = jnp.zeros((8, ch), F32)
        for shift in range(2 * NX):
            high, low = split(turned[shift:shift + width, :])
            s8th[:, shift * ch:(shift + 1) * ch] = high
            s8tl[:, shift * ch:(shift + 1) * ch] = low

    far_first = near_first(NZ)[::-1] + [0]

    def normal_start(it, image, hook=None):
        place = lax.broadcasted_iota(jnp.int32, (RB, width), 1)
        image = jnp.where(jnp.logical_and(place >= PAD, place < PAD + 2 * HALF), image, 0.0)
        moved = [image] + [pltpu.roll(image, 2 * NX * k, 1) for k in range(1, NZ)]
        high, low = split(jnp.concatenate(moved, axis=0))
        posts = {}
        for q in near_first(NX)[::-1] + [0]:
            if q == 0 and hook is not None:
                hook()
            xx = plus(x, q, NX)
            lanes_at = pl.ds(pl.multiple_of(xx * 2 * ch, 2 * ch), 2 * ch)
            main = s8th[:, lanes_at]
            part = mm(high, main) + mm(low, main) + mm(high, s8tl[:, lanes_at])
            zp[it, xx] = part.reshape(NZ, RB, 2 * ch)
            for o, k in enumerate(far_first if q else ()):
                i = slot()
                pending.append(start(zp.at[it, xx, plus(z, k, NZ)], rx.at[it, q - 1, o], dev(at(z, xx), core, y), i))
                posts[q, o] = i
        return it, posts, [slot() for _ in range(NZ)]

    def normal_relay(state, o):
        it, posts, back = state
        zz = plus(z, far_first[o], NZ)
        for q in range(1, NX):
            arrived(rx.at[it, q - 1, o], posts[q, o])
        total = zp[it, x, zz]
        for q in range(1, NX):
            total = total + rx[it, q - 1, o]
        zs[it, o] = total
        if far_first[o]:
            i = back[far_first[o]]
            pending.append(start(zs.at[it, o], rz.at[it, z], dev(at(zz, x), core, y), i))

    def normal_finish(state):
        it, _, back = state
        mine = zs[it, NZ - 1]
        for k in range(1, NZ):
            source = plus(z, NZ - k, NZ)
            arrived(rz.at[it, source], back[k])
            mine = mine + rz[it, source]
        return mine

    def share(src, ref_of):
        posts = []
        for dy, dc in peers[::-1]:
            i = slot()
            yy, cc = plus(y, dy, NY), plus(core, dc, 2)
            pending.append(start(src, ref_of(b), dev(t, cc, yy), i))
            posts.append((plus(y, NY - dy, NY) * 2 + plus(core, dc, 2), i))
        return ref_of, posts

    def shared(state):
        ref_of, posts = state
        for bb, i in posts[::-1]:
            arrived(ref_of(bb), i)

    def rows_share(it, chunk):
        pz[it, b] = chunk
        return share(pz.at[it, b], lambda bb: pz.at[it, bb])

    def along_z(it, product):
        gz[it, z] = product
        posts = []
        for k in near_first(NZ)[::-1]:
            i = slot()
            pending.append(start(gz.at[it, z], gz.at[it, z], dev(at(plus(z, k, NZ), x), core, y), i))
            posts.append((plus(z, NZ - k, NZ), i))
        return it, posts

    def along_x(state):
        it, posts = state
        for zz, i in posts[::-1]:
            arrived(gz.at[it, zz], i)
        total = gz[it, 0]
        for k in range(1, NZ):
            total = total + gz[it, k]
        gx[it, x] = total
        posts = []
        for k in near_first(NX)[::-1]:
            i = slot()
            pending.append(start(gx.at[it, x], gx.at[it, x], dev(at(z, plus(x, k, NX)), core, y), i))
            posts.append((plus(x, NX - k, NX), i))
        return it, posts

    def gram_share(state):
        it, posts = state
        for xx, i in posts[::-1]:
            arrived(gx.at[it, xx], i)
        total = gx[it, 0]
        for k in range(1, NX):
            total = total + gx[it, k]
        gp[it, b] = total
        return share(gp.at[it, b], lambda bb: gp.at[it, bb])

    def factor_start(it):
        line = lax.broadcasted_iota(jnp.int32, (rank, rank), 0)
        column = lax.broadcasted_iota(jnp.int32, (rank, rank), 1)
        aug[:, :rank] = gp[it].reshape(rank, rank)
        aug[:, rank:] = jnp.where(line == column, 1.0, 0.0).astype(F32)

    def factor_panels(it, low, high):
        sub = lax.broadcasted_iota(jnp.int32, (PANEL, rank), 0)

        def panel(k, carry):
            top = pl.multiple_of(k * PANEL, PANEL)
            left = aug[pl.ds(top, PANEL), :rank]
            right = aug[pl.ds(top, PANEL), rank:]
            turned = pltpu.roll(left, lax.rem(rank - k * PANEL, rank), 1)
            cols = [jnp.broadcast_to(turned[:, q:q + 1], (PANEL, rank)) for q in range(PANEL)]
            done_left = jnp.zeros((PANEL, rank), F32)
            done_right = done_left

            def line(value, p):
                return jnp.broadcast_to(value[p:p + 1, :], (PANEL, rank))

            for p in range(PANEL):
                root = lax.rsqrt(line(cols[p], p))
                step = cols[p] * root
                for q in range(p + 1, PANEL):
                    cols[q] = cols[q] - step * (line(cols[q], p) * root)
                left_line = line(left, p) * root
                right_line = line(right, p) * root
                done_left = jnp.where(sub == p, left_line, done_left)
                done_right = jnp.where(sub == p, right_line, done_right)
                left = left - step * left_line
                right = right - step * right_line
            both = jnp.concatenate([done_left, done_right], axis=1)
            fac[it, pl.ds(top, PANEL), :] = done_right
            aug[...] = aug[...] - exact(done_left, both, ((0,), (0,)))
            return carry

        lax.fori_loop(low, high, panel, 0)

    panels = rank // PANEL
    order = near_first(NZ)
    moving = gather_start(0, first_chunk)
    gather_relay(moving, order)
    setup_tile()
    gather_finish(moving)
    folding = normal_start(0, analyse(0))
    for o in range(NZ):
        normal_relay(folding, o)
    chunk = normal_finish(folding)

    moving = gather_start(1, chunk)
    joined = rows_share(0, chunk)
    gather_relay(moving, order[:2])
    shared(joined)
    gram = along_z(0, exact(pz[0, b], pz[0].reshape(rank, 2 * ch), ((1,), (1,))))
    gather_relay(moving, order[2:])
    early = (NX - 1) * (NZ // 2)
    gather_finish(moving, 0, early)
    gram = along_x(gram)
    gather_finish(moving, early)
    grams = []
    folding = normal_start(1, analyse(1), lambda: grams.append(gram_share(gram)))
    gram = grams[0]
    head = max(NZ - 5, 1)
    for o in range(head):
        normal_relay(folding, o)
    shared(gram)
    factor_start(0)
    for o in range(head, NZ):
        factor_panels(0, o - head, o - head + 1)
        normal_relay(folding, o)
    factor_panels(0, NZ - head, panels)
    chunk = normal_finish(folding)
    joined = rows_share(1, chunk)
    shared(joined)
    vfull[...] = exact(fac[0], pz[1].reshape(rank, 2 * ch)).reshape(blocks, RB, 2 * ch)

    chunk = vfull[b]
    gram = along_z(1, exact(chunk, vfull[...].reshape(rank, 2 * ch), ((1,), (1,))))
    moving = gather_start(2 + core, chunk)
    gather_relay(moving, order[:4])
    gram = along_x(gram)
    gather_relay(moving, order[4:])
    gram = gram_share(gram)
    gather_finish(moving)
    other = 1 - core
    swap = slot()
    pending.append(start(vall.at[2 + core], vall.at[2 + core], dev(t, other, y), swap))
    image = analyse(2 + core)
    for half in range(2):
        ys[half] = image[:, half * HALF:half * HALF + span]
    yx[b] = ys[core]
    posts = []
    for dy, dc in peers[::-1]:
        i = slot()
        yy, cc = plus(y, dy, NY), plus(core, dc, 2)
        pending.append(start(ys.at[cc], yx.at[b], dev(t, cc, yy), i))
        posts.append((plus(y, NY - dy, NY) * 2 + plus(core, dc, 2), i))
    joined = (lambda bb: yx.at[bb]), posts
    arrived(vall.at[2 + other], swap)
    both_blocks = jnp.concatenate([vall[2], vall[3]], axis=1).reshape(tiles * 2 * RB, 2 * ch)
    turned_high, turned_low = split(both_blocks.T)
    shared(gram)
    factor_start(1)
    factor_panels(1, 0, panels)
    inverse = fac[1]
    fac[0] = inverse.T
    weights = exact(fac[0, pl.ds(pl.multiple_of(y * 2 * RB, 2 * RB), 2 * RB), :], inverse)
    shared(joined)
    image = exact(weights, yx[...].reshape(rank, span))
    for i in range(tiles):
        high, low = split(image if i == 0 else pltpu.roll(image, 2 * i, 1))
        yh[i * 2 * RB:(i + 1) * 2 * RB, :] = high
        yl[i * 2 * RB:(i + 1) * 2 * RB, :] = low
    for bit in range(2):
        at_rows = slice(bit * ch, (bit + 1) * ch)
        part = (
            mm(turned_high[at_rows], yh[...])
            + mm(turned_low[at_rows], yh[...])
            + mm(turned_high[at_rows], yl[...])
        )
        if bit:
            total = total + pltpu.roll(part, 1, 1)
        else:
            total = part
    es[...] = total[:, PAD:].reshape(NY, CHG, HALF)
    back = []
    for dy in near_first(NY)[::-1]:
        j = slot()
        yy = plus(y, dy, NY)
        pending.append(start(es.at[yy], ey.at[dy], dev(t, core, yy), j))
        back.append((dy, j))
    estimate = es[y]
    both = exact(inverse, vfull[...].reshape(rank, 2 * ch))
    aug[:, :rank] = jnp.where(core == 0, both[:, :ch], both[:, ch:]).T
    bout_ref[...] = aug[pl.ds(pl.multiple_of(y * CHG, CHG), CHG), :rank]
    for dy, j in back:
        arrived(ey.at[dy], j)
        estimate = estimate + ey[dy]
    estimate = estimate * (1.0 / (2 * tiles))
    residual = mask_ref[...].astype(F32) * (ks_ref[...] - estimate)
    rec_ref[...] = estimate + residual - jnp.clip(residual, -THRESHOLD, THRESHOLD)
    for copy in pending + waiting:
        copy.wait_send()
    assert used[0] <= SEMS, used[0]


def shards(kspace, sample_mask, start_basis):
    tiles = NZ * NX
    ch = NY * CHG
    width = 2 * HALF + 2 * PAD
    span = HALF + PAD
    blocks = 2 * NY
    rank = blocks * RB
    vmem = pltpu.VMEM
    recovered, basis = pl.pallas_call(
        kernel,
        out_shape=(
            jax.ShapeDtypeStruct((CHG, HALF), F32),
            jax.ShapeDtypeStruct((CHG, rank), F32),
        ),
        in_specs=[pl.BlockSpec(memory_space=pltpu.HBM)] * 3,
        out_specs=(pl.BlockSpec(memory_space=pltpu.VMEM),) * 2,
        scratch_shapes=[
            vmem((CHG, HALF), F32),
            vmem((CHG, HALF), jnp.int32),
            vmem((CHG, rank), F32),
            vmem((CHG, HALF), F32),
            vmem((2, NY, CHG, HALF), F32),
            vmem((CHG, PAD), F32),
            vmem((2, NY, CHG, PAD), F32),
            vmem((blocks, RB, ch), F32),
            vmem((2, NY, RB, ch), F32),
            vmem((ITERS + 2, tiles, RB, 2 * ch), F32),
            vmem((2 * NX * ch, width), BF16),
            vmem((2 * NX * ch, width), BF16),
            vmem((width, 2 * NX * ch), BF16),
            vmem((width, 2 * NX * ch), BF16),
            vmem((width + 8, ch), F32),
            vmem((tiles * 2 * RB, span), BF16),
            vmem((tiles * 2 * RB, span), BF16),
            vmem((ITERS, NX, NZ, RB, 2 * ch), F32),
            vmem((ITERS, max(NX - 1, 1), NZ, RB, 2 * ch), F32),
            vmem((ITERS, NZ, RB, 2 * ch), F32),
            vmem((ITERS, NZ, RB, 2 * ch), F32),
            vmem((ITERS, blocks, RB, 2 * ch), F32),
            vmem((ITERS, NZ, RB, rank), F32),
            vmem((ITERS, NX, RB, rank), F32),
            vmem((ITERS, blocks, RB, rank), F32),
            vmem((rank, 2 * rank), F32),
            vmem((ITERS, rank, rank), F32),
            vmem((blocks, RB, 2 * ch), F32),
            vmem((2, RB, span), F32),
            vmem((blocks, RB, span), F32),
            vmem((NY, CHG, HALF), F32),
            vmem((NY, CHG, HALF), F32),
            pltpu.SemaphoreType.DMA((SEMS,)),
            pltpu.SemaphoreType.DMA((SEMS,)),
            pltpu.SemaphoreType.DMA((3,)),
        ],
        compiler_params=pltpu.CompilerParams(
            collective_id=0, has_side_effects=True, vmem_limit_bytes=67043328
        ),
    )(kspace, sample_mask, start_basis.reshape(CHG, rank))
    return recovered, basis.reshape(1, CHG, rank)


def solution(mesh):
    return jax.shard_map(
        shards,
        mesh=mesh,
        in_specs=(P("coil", "rows"), P("coil", "rows"), P("coil", "rows", None)),
        out_specs=(P("coil", "rows"), P("coil", "rows", None)),
        check_vma=False,
    )
```

```python
import functools

import jax
import jax.numpy as jnp
from jax import lax
from jax.experimental import pallas as pl
from jax.experimental.pallas import tpu as pltpu
from jax.sharding import PartitionSpec as P

NZ, NX, NY = 8, 4, 4
ITERS = 2
CHG = 32
HALF = 512
RB = 16
THRESHOLD = 0.05
MESH = pl.DeviceIdType.MESH
HIGHEST = lax.Precision.HIGHEST
F32 = jnp.float32
BF16 = jnp.bfloat16
PAD = 128
PANEL = 16
SEMS = 256


def split(value):
    high = value.astype(BF16)
    return high, (value - high.astype(F32)).astype(BF16)


def mm(a, b, dims=((1,), (0,))):
    return lax.dot_general(a, b, (dims, ((), ())), preferred_element_type=F32)


def exact(a, b, dims=((1,), (0,))):
    return lax.dot_general(
        a, b, (dims, ((), ())), precision=HIGHEST, preferred_element_type=F32
    )


def near_first(n):
    return sorted(range(1, n), key=lambda k: min(k, n - k))


def kernel(
    ks_hbm, mask_hbm, basis_hbm, rec_ref, bout_ref,
    ks_ref, mask_ref, basis_ref, own, sb, edge, halo, bt, vx, vall, s8h, s8l, s8th, s8tl, turned, yh, yl,
    zp, rx, zs, rz, pz, gz, gx, gp, aug, fac, vfull, ys, yx, es, ey,
    send, recv, load,
):
    loads = [
        pltpu.make_async_copy(src, dst, load.at[i])
        for i, (src, dst) in enumerate(
            ((basis_hbm, basis_ref), (ks_hbm, ks_ref), (mask_hbm, mask_ref))
        )
    ]
    for copy in loads:
        copy.start()
    tiles = NZ * NX
    ch = NY * CHG
    width = 2 * HALF + 2 * PAD
    span = HALF + PAD
    blocks = 2 * NY
    rank = blocks * RB
    rows = lax.axis_index("rows")
    y = lax.axis_index("coil")
    core = lax.rem(rows, 2)
    t = lax.div(rows, 2)
    x = lax.rem(t, NX)
    z = lax.div(t, NX)
    b = y * 2 + core
    used = [0]

    def dev(tile, c, yy):
        return (tile * 2 + c, yy)

    def slot():
        used[0] += 1
        return used[0] - 1

    def start(src, dst, device, i, j=None):
        copy = pltpu.make_async_remote_copy(
            src_ref=src, dst_ref=dst, send_sem=send.at[i],
            recv_sem=recv.at[i if j is None else j],
            device_id=device, device_id_type=MESH,
        )
        copy.start()
        return copy

    def arrived(dst, i):
        pltpu.make_async_remote_copy(
            src_ref=dst, dst_ref=dst, send_sem=send.at[i], recv_sem=recv.at[i],
            device_id=(rows, y), device_id_type=MESH,
        ).wait_recv()

    def at(zz, xx):
        return zz * NX + xx

    def plus(v, k, n):
        return lax.rem(v + k, n)

    ring = [(dy, dc) for dy in (0, 1, 3, 2) if dy < NY for dc in range(2)]
    peers = [p for p in ring if p != (0, 0)]
    before, after = plus(t, tiles - 1, tiles), plus(t, 1, tiles)

    barrier = pltpu.get_barrier_semaphore()
    greeted = 0
    for k in range(1, NZ):
        pl.semaphore_signal(barrier, inc=1, device_id=dev(at(plus(z, k, NZ), x), core, y), device_id_type=MESH)
        greeted += 1
    for k in range(1, NX):
        pl.semaphore_signal(barrier, inc=1, device_id=dev(at(z, plus(x, k, NX)), core, y), device_id_type=MESH)
        greeted += 1
    for dy, dc in peers:
        pl.semaphore_signal(barrier, inc=1, device_id=dev(t, plus(core, dc, 2), plus(y, dy, NY)), device_id_type=MESH)
        greeted += 1
    for tile in (before, after):
        for dy, dc in ring:
            pl.semaphore_signal(barrier, inc=1, device_id=dev(tile, plus(core, dc, 2), plus(y, dy, NY)), device_id_type=MESH)
            greeted += 1
    for copy in loads:
        copy.wait()
    lanes = lax.broadcasted_iota(jnp.int32, (rank, ch), 1)
    tiled = jnp.concatenate([basis_ref[...]] * NY, axis=0).T
    placed = jnp.where(lax.div(lanes, CHG) == y, tiled, 0.0)
    bt[...] = placed.reshape(blocks, RB, ch)
    sampled = ks_ref[...] * mask_ref[...].astype(F32)
    own[...] = sampled
    edge[...] = jnp.where(core == 0, sampled[:, :PAD], sampled[:, HALF - PAD:])
    pl.semaphore_wait(barrier, greeted)

    waiting = []
    basis_in = []
    for dy, dc in peers:
        i = slot()
        yy, cc = plus(y, dy, NY), plus(core, dc, 2)
        waiting.append(start(bt.at[yy * 2 + cc], vx.at[core, y], dev(t, cc, yy), i))
        basis_in.append((plus(core, dc, 2), plus(y, NY - dy, NY), i))
    tile_in = []
    for dy, dc in peers:
        i = slot()
        yy, cc = plus(y, dy, NY), plus(core, dc, 2)
        waiting.append(start(own, sb.at[core, y], dev(t, cc, yy), i))
        tile_in.append((plus(core, dc, 2), plus(y, NY - dy, NY), i))
    halo_base = [slot() for _ in range(2 * NY)]
    target = lax.rem(t + tiles + 2 * core - 1, tiles)
    for dy, dc in ring:
        i = halo_base[dc * NY + dy]
        yy, cc = plus(y, dy, NY), plus(core, dc, 2)
        waiting.append(start(edge, halo.at[core, y], dev(target, cc, yy), i, halo_base[0] + core * NY + dy))
    vx[core, y] = bt[b]
    sb[core, y] = own[...]
    for cc, yy, i in basis_in:
        arrived(vx.at[cc, yy], i)
    halves = []
    for half in range(2):
        total = vx[half, 0]
        for yy in range(1, NY):
            total = total + vx[half, yy]
        halves.append(total)
    first_chunk = jnp.concatenate(halves, axis=1)

    pending = []

    def gather_start(it, chunk):
        vall[it, t] = chunk
        first = {}
        for k in near_first(NZ):
            first[k] = slot()
            pending.append(start(vall.at[it, t], vall.at[it, t], dev(at(plus(z, k, NZ), x), core, y), first[k]))
        second = []
        gather_relay((it, first, second), (0,))
        return it, first, second

    def gather_relay(state, steps):
        it, first, second = state
        for k in steps:
            zz = plus(z, NZ - k, NZ)
            here = at(zz, x)
            if k:
                arrived(vall.at[it, here], first[k])
            for q in range(1, NX):
                i = slot()
                pending.append(start(vall.at[it, here], vall.at[it, here], dev(at(z, plus(x, q, NX)), core, y), i))
                second.append((at(zz, plus(x, NX - q, NX)), i))

    def gather_finish(state, low=0, high=None):
        for here, i in state[2][low:high]:
            arrived(vall.at[state[0], here], i)

    def analyse(it):
        slabs = vall[it].reshape(NZ, NX, RB, 2 * ch)
        joined = jnp.concatenate(
            [slabs[:, q].reshape(NZ * RB, 2 * ch) for q in range(NX)], axis=1
        )
        high, low = split(joined)
        size = NZ * RB
        main = mm(jnp.concatenate([high, low], axis=0), s8h[...])
        product = main[:size] + main[size:] + mm(high, s8l[...])
        image = product[0:RB]
        for k in range(1, NZ):
            image = image + pltpu.roll(product[k * RB:(k + 1) * RB], width - 2 * NX * k, 1)
        return image

    def setup_tile():
        for cc, yy, i in tile_in:
            arrived(sb.at[cc, yy], i)
        for s in range(2):
            for dy in range(NY):
                arrived(halo.at[s, plus(y, NY - dy, NY)], halo_base[s * NY + dy])
        full = jnp.concatenate(
            [
                jnp.concatenate([halo[1, g], sb[0, g], sb[1, g], halo[0, g]], axis=1)
                for g in range(NY)
            ],
            axis=0,
        )
        for shift in range(2 * NX):
            moved = full if shift == 0 else pltpu.roll(full, width - shift, 1)
            high, low = split(moved)
            s8h[shift * ch:(shift + 1) * ch, :] = high
            s8l[shift * ch:(shift + 1) * ch, :] = low
        turned[0:width, :] = full.T
        turned[width:width + 8, :] = jnp.zeros((8, ch), F32)
        for shift in range(2 * NX):
            high, low = split(turned[shift:shift + width, :])
            s8th[:, shift * ch:(shift + 1) * ch] = high
            s8tl[:, shift * ch:(shift + 1) * ch] = low

    far_first = near_first(NZ)[::-1] + [0]

    def normal_start(it, image, hook=None):
        place = lax.broadcasted_iota(jnp.int32, (RB, width), 1)
        image = jnp.where(jnp.logical_and(place >= PAD, place < PAD + 2 * HALF), image, 0.0)
        moved = [image] + [pltpu.roll(image, 2 * NX * k, 1) for k in range(1, NZ)]
        high, low = split(jnp.concatenate(moved, axis=0))
        stacked = jnp.concatenate([high, low], axis=0)
        size = NZ * RB
        posts = {}
        for q in near_first(NX)[::-1] + [0]:
            if q == 0 and hook is not None:
                hook()
            xx = plus(x, q, NX)
            lanes_at = pl.ds(pl.multiple_of(xx * 2 * ch, 2 * ch), 2 * ch)
            main = mm(stacked, s8th[:, lanes_at])
            part = main[:size] + main[size:] + mm(high, s8tl[:, lanes_at])
            zp[it, xx] = part.reshape(NZ, RB, 2 * ch)
            for o, k in enumerate(far_first if q else ()):
                i = slot()
                pending.append(start(zp.at[it, xx, plus(z, k, NZ)], rx.at[it, q - 1, o], dev(at(z, xx), core, y), i))
                posts[q, o] = i
        return it, posts, [slot() for _ in range(NZ)]

    def normal_relay(state, o):
        it, posts, back = state
        zz = plus(z, far_first[o], NZ)
        for q in range(1, NX):
            arrived(rx.at[it, q - 1, o], posts[q, o])
        total = zp[it, x, zz]
        for q in range(1, NX):
            total = total + rx[it, q - 1, o]
        zs[it, o] = total
        if far_first[o]:
            i = back[far_first[o]]
            pending.append(start(zs.at[it, o], rz.at[it, z], dev(at(zz, x), core, y), i))

    def normal_finish(state):
        it, _, back = state
        mine = zs[it, NZ - 1]
        for k in range(1, NZ):
            source = plus(z, NZ - k, NZ)
            arrived(rz.at[it, source], back[k])
            mine = mine + rz[it, source]
        return mine

    def share(src, ref_of):
        posts = []
        for dy, dc in peers[::-1]:
            i = slot()
            yy, cc = plus(y, dy, NY), plus(core, dc, 2)
            pending.append(start(src, ref_of(b), dev(t, cc, yy), i))
            posts.append((plus(y, NY - dy, NY) * 2 + plus(core, dc, 2), i))
        return ref_of, posts

    def shared(state):
        ref_of, posts = state
        for bb, i in posts[::-1]:
            arrived(ref_of(bb), i)

    def rows_share(it, chunk):
        pz[it, b] = chunk
        return share(pz.at[it, b], lambda bb: pz.at[it, bb])

    def along_z(it, product):
        gz[it, z] = product
        posts = []
        for k in near_first(NZ)[::-1]:
            i = slot()
            pending.append(start(gz.at[it, z], gz.at[it, z], dev(at(plus(z, k, NZ), x), core, y), i))
            posts.append((plus(z, NZ - k, NZ), i))
        return it, posts

    def along_x(state):
        it, posts = state
        for zz, i in posts[::-1]:
            arrived(gz.at[it, zz], i)
        total = gz[it, 0]
        for k in range(1, NZ):
            total = total + gz[it, k]
        gx[it, x] = total
        posts = []
        for k in near_first(NX)[::-1]:
            i = slot()
            pending.append(start(gx.at[it, x], gx.at[it, x], dev(at(z, plus(x, k, NX)), core, y), i))
            posts.append((plus(x, NX - k, NX), i))
        return it, posts

    def gram_share(state):
        it, posts = state
        for xx, i in posts[::-1]:
            arrived(gx.at[it, xx], i)
        total = gx[it, 0]
        for k in range(1, NX):
            total = total + gx[it, k]
        gp[it, b] = total
        return share(gp.at[it, b], lambda bb: gp.at[it, bb])

    def factor_start(it):
        line = lax.broadcasted_iota(jnp.int32, (rank, rank), 0)
        column = lax.broadcasted_iota(jnp.int32, (rank, rank), 1)
        aug[:, :rank] = gp[it].reshape(rank, rank)
        aug[:, rank:] = jnp.where(line == column, 1.0, 0.0).astype(F32)

    def factor_panels(it, low, high):
        sub = lax.broadcasted_iota(jnp.int32, (PANEL, rank), 0)

        def panel(k, carry):
            top = pl.multiple_of(k * PANEL, PANEL)
            left = aug[pl.ds(top, PANEL), :rank]
            right = aug[pl.ds(top, PANEL), rank:]
            turned = pltpu.roll(left, lax.rem(rank - k * PANEL, rank), 1)
            cols = [jnp.broadcast_to(turned[:, q:q + 1], (PANEL, rank)) for q in range(PANEL)]
            done_left = jnp.zeros((PANEL, rank), F32)
            done_right = done_left

            def line(value, p):
                return jnp.broadcast_to(value[p:p + 1, :], (PANEL, rank))

            for p in range(PANEL):
                root = lax.rsqrt(line(cols[p], p))
                step = cols[p] * root
                for q in range(p + 1, PANEL):
                    cols[q] = cols[q] - step * (line(cols[q], p) * root)
                left_line = line(left, p) * root
                right_line = line(right, p) * root
                done_left = jnp.where(sub == p, left_line, done_left)
                done_right = jnp.where(sub == p, right_line, done_right)
                left = left - step * left_line
                right = right - step * right_line
            both = jnp.concatenate([done_left, done_right], axis=1)
            fac[it, pl.ds(top, PANEL), :] = done_right
            aug[...] = aug[...] - exact(done_left, both, ((0,), (0,)))
            return carry

        lax.fori_loop(low, high, panel, 0)

    panels = rank // PANEL
    order = near_first(NZ)
    moving = gather_start(0, first_chunk)
    gather_relay(moving, order)
    setup_tile()
    gather_finish(moving)
    folding = normal_start(0, analyse(0))
    for o in range(NZ):
        normal_relay(folding, o)
    chunk = normal_finish(folding)

    moving = gather_start(1, chunk)
    joined = rows_share(0, chunk)
    gather_relay(moving, order[:2])
    shared(joined)
    gram = along_z(0, exact(pz[0, b], pz[0].reshape(rank, 2 * ch), ((1,), (1,))))
    gather_relay(moving, order[2:])
    early = (NX - 1) * (NZ // 2)
    gather_finish(moving, 0, early)
    gram = along_x(gram)
    gather_finish(moving, early)
    grams = []
    folding = normal_start(1, analyse(1), lambda: grams.append(gram_share(gram)))
    gram = grams[0]
    head = max(NZ - 5, 1)
    for o in range(head):
        normal_relay(folding, o)
    shared(gram)
    factor_start(0)
    for o in range(head, NZ):
        factor_panels(0, o - head, o - head + 1)
        normal_relay(folding, o)
    factor_panels(0, NZ - head, panels)
    chunk = normal_finish(folding)
    joined = rows_share(1, chunk)
    shared(joined)
    vfull[...] = exact(fac[0], pz[1].reshape(rank, 2 * ch)).reshape(blocks, RB, 2 * ch)

    chunk = vfull[b]
    gram = along_z(1, exact(chunk, vfull[...].reshape(rank, 2 * ch), ((1,), (1,))))
    moving = gather_start(2 + core, chunk)
    gather_relay(moving, order[:4])
    gram = along_x(gram)
    gather_relay(moving, order[4:])
    gram = gram_share(gram)
    gather_finish(moving)
    other = 1 - core
    swap = slot()
    pending.append(start(vall.at[2 + core], vall.at[2 + core], dev(t, other, y), swap))
    image = analyse(2 + core)
    for half in range(2):
        ys[half] = image[:, half * HALF:half * HALF + span]
    yx[b] = ys[core]
    posts = []
    for dy, dc in peers[::-1]:
        i = slot()
        yy, cc = plus(y, dy, NY), plus(core, dc, 2)
        pending.append(start(ys.at[cc], yx.at[b], dev(t, cc, yy), i))
        posts.append((plus(y, NY - dy, NY) * 2 + plus(core, dc, 2), i))
    joined = (lambda bb: yx.at[bb]), posts
    arrived(vall.at[2 + other], swap)
    both_blocks = jnp.concatenate([vall[2], vall[3]], axis=1).reshape(tiles * 2 * RB, 2 * ch)
    turned_high, turned_low = split(both_blocks.T)
    shared(gram)
    factor_start(1)
    factor_panels(1, 0, panels)
    inverse = fac[1]
    fac[0] = inverse.T
    weights = exact(fac[0, pl.ds(pl.multiple_of(y * 2 * RB, 2 * RB), 2 * RB), :], inverse)
    shared(joined)
    image = exact(weights, yx[...].reshape(rank, span))
    for i in range(tiles):
        high, low = split(image if i == 0 else pltpu.roll(image, 2 * i, 1))
        yh[i * 2 * RB:(i + 1) * 2 * RB, :] = high
        yl[i * 2 * RB:(i + 1) * 2 * RB, :] = low
    main = mm(jnp.concatenate([turned_high, turned_low], axis=0), yh[...])
    part = main[:2 * ch] + main[2 * ch:] + mm(turned_high, yl[...])
    total = part[:ch] + pltpu.roll(part[ch:], 1, 1)
    es[...] = total[:, PAD:].reshape(NY, CHG, HALF)
    back = []
    for dy in near_first(NY)[::-1]:
        j = slot()
        yy = plus(y, dy, NY)
        pending.append(start(es.at[yy], ey.at[dy], dev(t, core, yy), j))
        back.append((dy, j))
    estimate = es[y]
    both = exact(inverse, vfull[...].reshape(rank, 2 * ch))
    aug[:, :rank] = jnp.where(core == 0, both[:, :ch], both[:, ch:]).T
    bout_ref[...] = aug[pl.ds(pl.multiple_of(y * CHG, CHG), CHG), :rank]
    for copy in waiting + pending[:-(NY - 1)]:
        copy.wait_send()
    for dy, j in back:
        arrived(ey.at[dy], j)
        estimate = estimate + ey[dy]
    estimate = estimate * (1.0 / (2 * tiles))
    residual = mask_ref[...].astype(F32) * (ks_ref[...] - estimate)
    rec_ref[...] = estimate + residual - jnp.clip(residual, -THRESHOLD, THRESHOLD)
    for copy in pending[-(NY - 1):]:
        copy.wait_send()
    assert used[0] <= SEMS, used[0]


def shards(kspace, sample_mask, start_basis):
    tiles = NZ * NX
    ch = NY * CHG
    width = 2 * HALF + 2 * PAD
    span = HALF + PAD
    blocks = 2 * NY
    rank = blocks * RB
    vmem = pltpu.VMEM
    operands = (kspace, sample_mask, start_basis.reshape(CHG, rank))
    recovered, basis = pl.pallas_call(
        kernel,
        out_shape=(
            jax.ShapeDtypeStruct((CHG, HALF), F32),
            jax.ShapeDtypeStruct((CHG, rank), F32),
        ),
        in_specs=[pl.BlockSpec(memory_space=pltpu.HBM)] * 3,
        out_specs=(pl.BlockSpec(memory_space=pltpu.VMEM),) * 2,
        scratch_shapes=[
            vmem((CHG, HALF), F32),
            vmem((CHG, HALF), jnp.int32),
            vmem((CHG, rank), F32),
            vmem((CHG, HALF), F32),
            vmem((2, NY, CHG, HALF), F32),
            vmem((CHG, PAD), F32),
            vmem((2, NY, CHG, PAD), F32),
            vmem((blocks, RB, ch), F32),
            vmem((2, NY, RB, ch), F32),
            vmem((ITERS + 2, tiles, RB, 2 * ch), F32),
            vmem((2 * NX * ch, width), BF16),
            vmem((2 * NX * ch, width), BF16),
            vmem((width, 2 * NX * ch), BF16),
            vmem((width, 2 * NX * ch), BF16),
            vmem((width + 8, ch), F32),
            vmem((tiles * 2 * RB, span), BF16),
            vmem((tiles * 2 * RB, span), BF16),
            vmem((ITERS, NX, NZ, RB, 2 * ch), F32),
            vmem((ITERS, max(NX - 1, 1), NZ, RB, 2 * ch), F32),
            vmem((ITERS, NZ, RB, 2 * ch), F32),
            vmem((ITERS, NZ, RB, 2 * ch), F32),
            vmem((ITERS, blocks, RB, 2 * ch), F32),
            vmem((ITERS, NZ, RB, rank), F32),
            vmem((ITERS, NX, RB, rank), F32),
            vmem((ITERS, blocks, RB, rank), F32),
            vmem((rank, 2 * rank), F32),
            vmem((ITERS, rank, rank), F32),
            vmem((blocks, RB, 2 * ch), F32),
            vmem((2, RB, span), F32),
            vmem((blocks, RB, span), F32),
            vmem((NY, CHG, HALF), F32),
            vmem((NY, CHG, HALF), F32),
            pltpu.SemaphoreType.DMA((SEMS,)),
            pltpu.SemaphoreType.DMA((SEMS,)),
            pltpu.SemaphoreType.DMA((3,)),
        ],
        compiler_params=pltpu.CompilerParams(
            collective_id=0, has_side_effects=True, vmem_limit_bytes=48 << 20
        ),
    )(*[pltpu.with_memory_space_constraint(v, pltpu.HBM) for v in operands])
    return recovered, basis.reshape(1, CHG, rank)


def solution(mesh):
    return jax.shard_map(
        shards,
        mesh=mesh,
        in_specs=(P("coil", "rows"), P("coil", "rows"), P("coil", "rows", None)),
        out_specs=(P("coil", "rows"), P("coil", "rows", None)),
        check_vma=False,
    )
```

```python
import functools

import jax
import jax.numpy as jnp
from jax import lax
from jax.experimental import pallas as pl
from jax.experimental.pallas import tpu as pltpu
from jax.sharding import PartitionSpec as P

NZ, NX, NY = 8, 4, 4
ITERS = 2
CHG = 32
HALF = 512
RB = 16
THRESHOLD = 0.05
MESH = pl.DeviceIdType.MESH
HIGHEST = lax.Precision.HIGHEST
F32 = jnp.float32
BF16 = jnp.bfloat16
PAD = 128
PANEL = 16
SEMS = 256


def split(value):
    high = value.astype(BF16)
    return high, (value - high.astype(F32)).astype(BF16)


def mm(a, b, dims=((1,), (0,))):
    return lax.dot_general(a, b, (dims, ((), ())), preferred_element_type=F32)


def exact(a, b, dims=((1,), (0,))):
    return lax.dot_general(
        a, b, (dims, ((), ())), precision=HIGHEST, preferred_element_type=F32
    )


def near_first(n):
    return sorted(range(1, n), key=lambda k: min(k, n - k))


def kernel(
    ks_hbm, mask_hbm, basis_hbm, rec_ref, bout_ref,
    ks_ref, mask_ref, basis_ref, own, sb, edge, halo, bt, vx, vall, s8h, s8l, s8th, s8tl, turned, yh, yl,
    zp, rx, zs, rz, pz, gz, gx, gp, aug, fac, vfull, ys, yx, es, ey,
    send, recv, load,
):
    loads = [
        pltpu.make_async_copy(src, dst, load.at[i])
        for i, (src, dst) in enumerate(
            ((basis_hbm, basis_ref), (ks_hbm, ks_ref), (mask_hbm, mask_ref))
        )
    ]
    for copy in loads:
        copy.start()
    tiles = NZ * NX
    ch = NY * CHG
    width = 2 * HALF + 2 * PAD
    span = HALF + PAD
    blocks = 2 * NY
    rank = blocks * RB
    rows = lax.axis_index("rows")
    y = lax.axis_index("coil")
    core = lax.rem(rows, 2)
    t = lax.div(rows, 2)
    x = lax.rem(t, NX)
    z = lax.div(t, NX)
    b = y * 2 + core
    used = [0]

    def dev(tile, c, yy):
        return (tile * 2 + c, yy)

    def slot():
        used[0] += 1
        return used[0] - 1

    def start(src, dst, device, i, j=None):
        copy = pltpu.make_async_remote_copy(
            src_ref=src, dst_ref=dst, send_sem=send.at[i],
            recv_sem=recv.at[i if j is None else j],
            device_id=device, device_id_type=MESH,
        )
        copy.start()
        return copy

    def arrived(dst, i):
        pltpu.make_async_remote_copy(
            src_ref=dst, dst_ref=dst, send_sem=send.at[i], recv_sem=recv.at[i],
            device_id=(rows, y), device_id_type=MESH,
        ).wait_recv()

    def at(zz, xx):
        return zz * NX + xx

    def plus(v, k, n):
        return lax.rem(v + k, n)

    ring = [(dy, dc) for dy in (0, 1, 3, 2) if dy < NY for dc in range(2)]
    peers = [p for p in ring if p != (0, 0)]
    before, after = plus(t, tiles - 1, tiles), plus(t, 1, tiles)

    barrier = pltpu.get_barrier_semaphore()
    greeted = 0
    for k in range(1, NZ):
        pl.semaphore_signal(barrier, inc=1, device_id=dev(at(plus(z, k, NZ), x), core, y), device_id_type=MESH)
        greeted += 1
    for k in range(1, NX):
        pl.semaphore_signal(barrier, inc=1, device_id=dev(at(z, plus(x, k, NX)), core, y), device_id_type=MESH)
        greeted += 1
    for dy, dc in peers:
        pl.semaphore_signal(barrier, inc=1, device_id=dev(t, plus(core, dc, 2), plus(y, dy, NY)), device_id_type=MESH)
        greeted += 1
    for tile in (before, after):
        for dy, dc in ring:
            pl.semaphore_signal(barrier, inc=1, device_id=dev(tile, plus(core, dc, 2), plus(y, dy, NY)), device_id_type=MESH)
            greeted += 1
    for copy in loads:
        copy.wait()
    lanes = lax.broadcasted_iota(jnp.int32, (rank, ch), 1)
    tiled = jnp.concatenate([basis_ref[...]] * NY, axis=0).T
    placed = jnp.where(lax.div(lanes, CHG) == y, tiled, 0.0)
    bt[...] = placed.reshape(blocks, RB, ch)
    sampled = ks_ref[...] * mask_ref[...].astype(F32)
    own[...] = sampled
    edge[...] = jnp.where(core == 0, sampled[:, :PAD], sampled[:, HALF - PAD:])
    pl.semaphore_wait(barrier, greeted)

    waiting = []
    basis_in = []
    for dy, dc in peers:
        i = slot()
        yy, cc = plus(y, dy, NY), plus(core, dc, 2)
        waiting.append(start(bt.at[yy * 2 + cc], vx.at[core, y], dev(t, cc, yy), i))
        basis_in.append((plus(core, dc, 2), plus(y, NY - dy, NY), i))
    tile_in = []
    for dy, dc in peers:
        i = slot()
        yy, cc = plus(y, dy, NY), plus(core, dc, 2)
        waiting.append(start(own, sb.at[core, y], dev(t, cc, yy), i))
        tile_in.append((plus(core, dc, 2), plus(y, NY - dy, NY), i))
    halo_base = [slot() for _ in range(2 * NY)]
    target = lax.rem(t + tiles + 2 * core - 1, tiles)
    for dy, dc in ring:
        i = halo_base[dc * NY + dy]
        yy, cc = plus(y, dy, NY), plus(core, dc, 2)
        waiting.append(start(edge, halo.at[core, y], dev(target, cc, yy), i, halo_base[0] + core * NY + dy))
    vx[core, y] = bt[b]
    sb[core, y] = own[...]
    for cc, yy, i in basis_in:
        arrived(vx.at[cc, yy], i)
    halves = []
    for half in range(2):
        total = vx[half, 0]
        for yy in range(1, NY):
            total = total + vx[half, yy]
        halves.append(total)
    first_chunk = jnp.concatenate(halves, axis=1)

    pending = []

    def gather_start(it, chunk):
        vall[it, t] = chunk
        first = {}
        for k in near_first(NZ):
            first[k] = slot()
            pending.append(start(vall.at[it, t], vall.at[it, t], dev(at(plus(z, k, NZ), x), core, y), first[k]))
        second = []
        gather_relay((it, first, second), (0,))
        return it, first, second

    def gather_relay(state, steps):
        it, first, second = state
        for k in steps:
            zz = plus(z, NZ - k, NZ)
            here = at(zz, x)
            if k:
                arrived(vall.at[it, here], first[k])
            for q in range(1, NX):
                i = slot()
                pending.append(start(vall.at[it, here], vall.at[it, here], dev(at(z, plus(x, q, NX)), core, y), i))
                second.append((at(zz, plus(x, NX - q, NX)), i))

    def gather_finish(state, low=0, high=None):
        for here, i in state[2][low:high]:
            arrived(vall.at[state[0], here], i)

    def analyse(it, first=False):
        slabs = vall[it].reshape(NZ, NX, RB, 2 * ch)
        joined = jnp.concatenate(
            [slabs[:, q].reshape(NZ * RB, 2 * ch) for q in range(NX)], axis=1
        )
        high, low = split(joined)
        size = NZ * RB
        stacked = jnp.concatenate([high, low], axis=0)
        if first:
            main = mm(stacked, s8th[...], ((1,), (1,)))
            product = main[:size] + main[size:] + mm(high, s8tl[...], ((1,), (1,)))
        else:
            main = mm(stacked, s8h[...])
            product = main[:size] + main[size:] + mm(high, s8l[...])
        image = product[0:RB]
        for k in range(1, NZ):
            image = image + pltpu.roll(product[k * RB:(k + 1) * RB], width - 2 * NX * k, 1)
        return image

    def whole_tile():
        return jnp.concatenate(
            [
                jnp.concatenate([halo[1, g], sb[0, g], sb[1, g], halo[0, g]], axis=1)
                for g in range(NY)
            ],
            axis=0,
        )

    def setup_rows():
        full = whole_tile()
        for shift in range(2 * NX):
            moved = full if shift == 0 else pltpu.roll(full, width - shift, 1)
            high, low = split(moved)
            s8h[shift * ch:(shift + 1) * ch, :] = high
            s8l[shift * ch:(shift + 1) * ch, :] = low

    def setup_tile():
        for cc, yy, i in tile_in:
            arrived(sb.at[cc, yy], i)
        for s in range(2):
            for dy in range(NY):
                arrived(halo.at[s, plus(y, NY - dy, NY)], halo_base[s * NY + dy])
        turned[0:width, :] = whole_tile().T
        turned[width:width + 8, :] = jnp.zeros((8, ch), F32)
        for shift in range(2 * NX):
            high, low = split(turned[shift:shift + width, :])
            s8th[:, shift * ch:(shift + 1) * ch] = high
            s8tl[:, shift * ch:(shift + 1) * ch] = low

    far_first = near_first(NZ)[::-1] + [0]

    def normal_start(it, image, hook=None):
        place = lax.broadcasted_iota(jnp.int32, (RB, width), 1)
        image = jnp.where(jnp.logical_and(place >= PAD, place < PAD + 2 * HALF), image, 0.0)
        moved = [image] + [pltpu.roll(image, 2 * NX * k, 1) for k in range(1, NZ)]
        high, low = split(jnp.concatenate(moved, axis=0))
        stacked = jnp.concatenate([high, low], axis=0)
        size = NZ * RB
        posts = {}
        for q in near_first(NX)[::-1] + [0]:
            if q == 0 and hook is not None:
                hook()
            xx = plus(x, q, NX)
            lanes_at = pl.ds(pl.multiple_of(xx * 2 * ch, 2 * ch), 2 * ch)
            main = mm(stacked, s8th[:, lanes_at])
            part = main[:size] + main[size:] + mm(high, s8tl[:, lanes_at])
            zp[it, xx] = part.reshape(NZ, RB, 2 * ch)
            for o, k in enumerate(far_first if q else ()):
                i = slot()
                pending.append(start(zp.at[it, xx, plus(z, k, NZ)], rx.at[it, q - 1, o], dev(at(z, xx), core, y), i))
                posts[q, o] = i
        return it, posts, [slot() for _ in range(NZ)]

    def normal_relay(state, o):
        it, posts, back = state
        zz = plus(z, far_first[o], NZ)
        for q in range(1, NX):
            arrived(rx.at[it, q - 1, o], posts[q, o])
        total = zp[it, x, zz]
        for q in range(1, NX):
            total = total + rx[it, q - 1, o]
        zs[it, o] = total
        if far_first[o]:
            i = back[far_first[o]]
            pending.append(start(zs.at[it, o], rz.at[it, z], dev(at(zz, x), core, y), i))

    def normal_finish(state):
        it, _, back = state
        mine = zs[it, NZ - 1]
        for k in range(1, NZ):
            source = plus(z, NZ - k, NZ)
            arrived(rz.at[it, source], back[k])
            mine = mine + rz[it, source]
        return mine

    def share(src, ref_of):
        posts = []
        for dy, dc in peers[::-1]:
            i = slot()
            yy, cc = plus(y, dy, NY), plus(core, dc, 2)
            pending.append(start(src, ref_of(b), dev(t, cc, yy), i))
            posts.append((plus(y, NY - dy, NY) * 2 + plus(core, dc, 2), i))
        return ref_of, posts

    def shared(state):
        ref_of, posts = state
        for bb, i in posts[::-1]:
            arrived(ref_of(bb), i)

    def rows_share(it, chunk):
        pz[it, b] = chunk
        return share(pz.at[it, b], lambda bb: pz.at[it, bb])

    def along_z(it, product):
        gz[it, z] = product
        posts = []
        for k in near_first(NZ)[::-1]:
            i = slot()
            pending.append(start(gz.at[it, z], gz.at[it, z], dev(at(plus(z, k, NZ), x), core, y), i))
            posts.append((plus(z, NZ - k, NZ), i))
        return it, posts

    def along_x(state):
        it, posts = state
        for zz, i in posts[::-1]:
            arrived(gz.at[it, zz], i)
        total = gz[it, 0]
        for k in range(1, NZ):
            total = total + gz[it, k]
        gx[it, x] = total
        posts = []
        for k in near_first(NX)[::-1]:
            i = slot()
            pending.append(start(gx.at[it, x], gx.at[it, x], dev(at(z, plus(x, k, NX)), core, y), i))
            posts.append((plus(x, NX - k, NX), i))
        return it, posts

    def gram_share(state):
        it, posts = state
        for xx, i in posts[::-1]:
            arrived(gx.at[it, xx], i)
        total = gx[it, 0]
        for k in range(1, NX):
            total = total + gx[it, k]
        gp[it, b] = total
        return share(gp.at[it, b], lambda bb: gp.at[it, bb])

    def factor_start(it):
        line = lax.broadcasted_iota(jnp.int32, (rank, rank), 0)
        column = lax.broadcasted_iota(jnp.int32, (rank, rank), 1)
        aug[:, :rank] = gp[it].reshape(rank, rank)
        aug[:, rank:] = jnp.where(line == column, 1.0, 0.0).astype(F32)

    def factor_panels(it, low, high):
        sub = lax.broadcasted_iota(jnp.int32, (PANEL, rank), 0)

        def panel(k, carry):
            top = pl.multiple_of(k * PANEL, PANEL)
            left = aug[pl.ds(top, PANEL), :rank]
            right = aug[pl.ds(top, PANEL), rank:]
            turned = pltpu.roll(left, lax.rem(rank - k * PANEL, rank), 1)
            cols = [jnp.broadcast_to(turned[:, q:q + 1], (PANEL, rank)) for q in range(PANEL)]
            done_left = jnp.zeros((PANEL, rank), F32)
            done_right = done_left

            def line(value, p):
                return jnp.broadcast_to(value[p:p + 1, :], (PANEL, rank))

            for p in range(PANEL):
                root = lax.rsqrt(line(cols[p], p))
                step = cols[p] * root
                for q in range(p + 1, PANEL):
                    cols[q] = cols[q] - step * (line(cols[q], p) * root)
                left_line = line(left, p) * root
                right_line = line(right, p) * root
                done_left = jnp.where(sub == p, left_line, done_left)
                done_right = jnp.where(sub == p, right_line, done_right)
                left = left - step * left_line
                right = right - step * right_line
            both = jnp.concatenate([done_left, done_right], axis=1)
            fac[it, pl.ds(top, PANEL), :] = done_right
            aug[...] = aug[...] - exact(done_left, both, ((0,), (0,)))
            return carry

        lax.fori_loop(low, high, panel, 0)

    panels = rank // PANEL
    order = near_first(NZ)
    moving = gather_start(0, first_chunk)
    gather_relay(moving, order)
    setup_tile()
    gather_finish(moving)
    folding = normal_start(0, analyse(0, True))
    setup_rows()
    for o in range(NZ):
        normal_relay(folding, o)
    chunk = normal_finish(folding)

    moving = gather_start(1, chunk)
    joined = rows_share(0, chunk)
    gather_relay(moving, order[:2])
    shared(joined)
    gram = along_z(0, exact(pz[0, b], pz[0].reshape(rank, 2 * ch), ((1,), (1,))))
    gather_relay(moving, order[2:])
    early = (NX - 1) * (NZ // 2)
    gather_finish(moving, 0, early)
    gram = along_x(gram)
    gather_finish(moving, early)
    grams = []
    folding = normal_start(1, analyse(1), lambda: grams.append(gram_share(gram)))
    gram = grams[0]
    head = max(NZ - 5, 1)
    for o in range(head):
        normal_relay(folding, o)
    shared(gram)
    factor_start(0)
    for o in range(head, NZ):
        factor_panels(0, o - head, o - head + 1)
        normal_relay(folding, o)
    factor_panels(0, NZ - head, panels)
    chunk = normal_finish(folding)
    joined = rows_share(1, chunk)
    shared(joined)
    vfull[...] = exact(fac[0], pz[1].reshape(rank, 2 * ch)).reshape(blocks, RB, 2 * ch)

    chunk = vfull[b]
    gram = along_z(1, exact(chunk, vfull[...].reshape(rank, 2 * ch), ((1,), (1,))))
    moving = gather_start(2 + core, chunk)
    gather_relay(moving, order[:4])
    gram = along_x(gram)
    gather_relay(moving, order[4:])
    gram = gram_share(gram)
    gather_finish(moving)
    other = 1 - core
    swap = slot()
    pending.append(start(vall.at[2 + core], vall.at[2 + core], dev(t, other, y), swap))
    image = analyse(2 + core)
    for half in range(2):
        ys[half] = image[:, half * HALF:half * HALF + span]
    yx[b] = ys[core]
    posts = []
    for dy, dc in peers[::-1]:
        i = slot()
        yy, cc = plus(y, dy, NY), plus(core, dc, 2)
        pending.append(start(ys.at[cc], yx.at[b], dev(t, cc, yy), i))
        posts.append((plus(y, NY - dy, NY) * 2 + plus(core, dc, 2), i))
    joined = (lambda bb: yx.at[bb]), posts
    arrived(vall.at[2 + other], swap)
    both_blocks = jnp.concatenate([vall[2], vall[3]], axis=1).reshape(tiles * 2 * RB, 2 * ch)
    turned_high, turned_low = split(both_blocks.T)
    shared(gram)
    factor_start(1)
    factor_panels(1, 0, panels)
    inverse = fac[1]
    fac[0] = inverse.T
    weights = exact(fac[0, pl.ds(pl.multiple_of(y * 2 * RB, 2 * RB), 2 * RB), :], inverse)
    shared(joined)
    high, low = split(weights)
    wide_high, wide_low = split(yx[...].reshape(rank, span))
    main = mm(jnp.concatenate([high, low], axis=0), wide_high)
    image = main[:2 * RB] + main[2 * RB:] + mm(high, wide_low)
    for i in range(tiles):
        high, low = split(image if i == 0 else pltpu.roll(image, 2 * i, 1))
        yh[i * 2 * RB:(i + 1) * 2 * RB, :] = high
        yl[i * 2 * RB:(i + 1) * 2 * RB, :] = low
    main = mm(jnp.concatenate([turned_high, turned_low], axis=0), yh[...])
    part = main[:2 * ch] + main[2 * ch:] + mm(turned_high, yl[...])
    total = part[:ch] + pltpu.roll(part[ch:], 1, 1)
    es[...] = total[:, PAD:].reshape(NY, CHG, HALF)
    back = []
    for dy in near_first(NY)[::-1]:
        j = slot()
        yy = plus(y, dy, NY)
        pending.append(start(es.at[yy], ey.at[dy], dev(t, core, yy), j))
        back.append((dy, j))
    estimate = es[y]
    both = exact(inverse, vfull[...].reshape(rank, 2 * ch))
    aug[:, :rank] = jnp.where(core == 0, both[:, :ch], both[:, ch:]).T
    bout_ref[...] = aug[pl.ds(pl.multiple_of(y * CHG, CHG), CHG), :rank]
    for copy in waiting + pending[:-(NY - 1)]:
        copy.wait_send()
    for dy, j in back:
        arrived(ey.at[dy], j)
        estimate = estimate + ey[dy]
    estimate = estimate * (1.0 / (2 * tiles))
    residual = mask_ref[...].astype(F32) * (ks_ref[...] - estimate)
    rec_ref[...] = estimate + residual - jnp.clip(residual, -THRESHOLD, THRESHOLD)
    for copy in pending[-(NY - 1):]:
        copy.wait_send()
    assert used[0] <= SEMS, used[0]


def shards(kspace, sample_mask, start_basis):
    tiles = NZ * NX
    ch = NY * CHG
    width = 2 * HALF + 2 * PAD
    span = HALF + PAD
    blocks = 2 * NY
    rank = blocks * RB
    vmem = pltpu.VMEM
    operands = (kspace, sample_mask, start_basis.reshape(CHG, rank))
    recovered, basis = pl.pallas_call(
        kernel,
        out_shape=(
            jax.ShapeDtypeStruct((CHG, HALF), F32),
            jax.ShapeDtypeStruct((CHG, rank), F32),
        ),
        in_specs=[pl.BlockSpec(memory_space=pltpu.HBM)] * 3,
        out_specs=(pl.BlockSpec(memory_space=pltpu.VMEM),) * 2,
        scratch_shapes=[
            vmem((CHG, HALF), F32),
            vmem((CHG, HALF), jnp.int32),
            vmem((CHG, rank), F32),
            vmem((CHG, HALF), F32),
            vmem((2, NY, CHG, HALF), F32),
            vmem((CHG, PAD), F32),
            vmem((2, NY, CHG, PAD), F32),
            vmem((blocks, RB, ch), F32),
            vmem((2, NY, RB, ch), F32),
            vmem((ITERS + 2, tiles, RB, 2 * ch), F32),
            vmem((2 * NX * ch, width), BF16),
            vmem((2 * NX * ch, width), BF16),
            vmem((width, 2 * NX * ch), BF16),
            vmem((width, 2 * NX * ch), BF16),
            vmem((width + 8, ch), F32),
            vmem((tiles * 2 * RB, span), BF16),
            vmem((tiles * 2 * RB, span), BF16),
            vmem((ITERS, NX, NZ, RB, 2 * ch), F32),
            vmem((ITERS, max(NX - 1, 1), NZ, RB, 2 * ch), F32),
            vmem((ITERS, NZ, RB, 2 * ch), F32),
            vmem((ITERS, NZ, RB, 2 * ch), F32),
            vmem((ITERS, blocks, RB, 2 * ch), F32),
            vmem((ITERS, NZ, RB, rank), F32),
            vmem((ITERS, NX, RB, rank), F32),
            vmem((ITERS, blocks, RB, rank), F32),
            vmem((rank, 2 * rank), F32),
            vmem((ITERS, rank, rank), F32),
            vmem((blocks, RB, 2 * ch), F32),
            vmem((2, RB, span), F32),
            vmem((blocks, RB, span), F32),
            vmem((NY, CHG, HALF), F32),
            vmem((NY, CHG, HALF), F32),
            pltpu.SemaphoreType.DMA((SEMS,)),
            pltpu.SemaphoreType.DMA((SEMS,)),
            pltpu.SemaphoreType.DMA((3,)),
        ],
        compiler_params=pltpu.CompilerParams(
            collective_id=0, has_side_effects=True, vmem_limit_bytes=48 << 20
        ),
    )(*[pltpu.with_memory_space_constraint(v, pltpu.HBM) for v in operands])
    return recovered, basis.reshape(1, CHG, rank)


def solution(mesh):
    return jax.shard_map(
        shards,
        mesh=mesh,
        in_specs=(P("coil", "rows"), P("coil", "rows"), P("coil", "rows", None)),
        out_specs=(P("coil", "rows"), P("coil", "rows", None)),
        check_vma=False,
    )
```

```python
import functools

import jax
import jax.numpy as jnp
from jax import lax
from jax.experimental import pallas as pl
from jax.experimental.pallas import tpu as pltpu
from jax.sharding import PartitionSpec as P

NZ, NX, NY = 8, 4, 4
ITERS = 2
CHG = 32
HALF = 512
RB = 16
THRESHOLD = 0.05
MESH = pl.DeviceIdType.MESH
HIGHEST = lax.Precision.HIGHEST
F32 = jnp.float32
BF16 = jnp.bfloat16
PAD = 128
PANEL = 16
SEMS = 256


def split(value):
    high = value.astype(BF16)
    return high, (value - high.astype(F32)).astype(BF16)


def mm(a, b, dims=((1,), (0,))):
    return lax.dot_general(a, b, (dims, ((), ())), preferred_element_type=F32)


def exact(a, b, dims=((1,), (0,))):
    return lax.dot_general(
        a, b, (dims, ((), ())), precision=HIGHEST, preferred_element_type=F32
    )


def near_first(n):
    return sorted(range(1, n), key=lambda k: min(k, n - k))


def kernel(
    ks_hbm, mask_hbm, basis_hbm, rec_ref, bout_ref,
    ks_ref, mask_ref, basis_ref, own, sb, edge, halo, bt, vx, vall, s8h, s8l, s8th, s8tl, turned, yh, yl,
    zp, rx, zs, rz, pz, gz, gx, gp, aug, fac, vfull, ys, yx, es, ey,
    send, recv, load,
):
    loads = [
        pltpu.make_async_copy(src, dst, load.at[i])
        for i, (src, dst) in enumerate(
            ((basis_hbm, basis_ref), (ks_hbm, ks_ref), (mask_hbm, mask_ref))
        )
    ]
    for copy in loads:
        copy.start()
    tiles = NZ * NX
    ch = NY * CHG
    width = 2 * HALF + 2 * PAD
    span = HALF + PAD
    blocks = 2 * NY
    rank = blocks * RB
    rows = lax.axis_index("rows")
    y = lax.axis_index("coil")
    core = lax.rem(rows, 2)
    t = lax.div(rows, 2)
    x = lax.rem(t, NX)
    z = lax.div(t, NX)
    b = y * 2 + core
    used = [0]

    def dev(tile, c, yy):
        return (tile * 2 + c, yy)

    def slot():
        used[0] += 1
        return used[0] - 1

    def start(src, dst, device, i, j=None):
        copy = pltpu.make_async_remote_copy(
            src_ref=src, dst_ref=dst, send_sem=send.at[i],
            recv_sem=recv.at[i if j is None else j],
            device_id=device, device_id_type=MESH,
        )
        copy.start()
        return copy

    def arrived(dst, i):
        pltpu.make_async_remote_copy(
            src_ref=dst, dst_ref=dst, send_sem=send.at[i], recv_sem=recv.at[i],
            device_id=(rows, y), device_id_type=MESH,
        ).wait_recv()

    def at(zz, xx):
        return zz * NX + xx

    def plus(v, k, n):
        return lax.rem(v + k, n)

    ring = [(dy, dc) for dy in (0, 1, 3, 2) if dy < NY for dc in range(2)]
    peers = [p for p in ring if p != (0, 0)]
    before, after = plus(t, tiles - 1, tiles), plus(t, 1, tiles)

    barrier = pltpu.get_barrier_semaphore()
    greeted = 0
    for k in range(1, NZ):
        pl.semaphore_signal(barrier, inc=1, device_id=dev(at(plus(z, k, NZ), x), core, y), device_id_type=MESH)
        greeted += 1
    for k in range(1, NX):
        pl.semaphore_signal(barrier, inc=1, device_id=dev(at(z, plus(x, k, NX)), core, y), device_id_type=MESH)
        greeted += 1
    for dy, dc in peers:
        pl.semaphore_signal(barrier, inc=1, device_id=dev(t, plus(core, dc, 2), plus(y, dy, NY)), device_id_type=MESH)
        greeted += 1
    for tile in (before, after):
        for dy, dc in ring:
            pl.semaphore_signal(barrier, inc=1, device_id=dev(tile, plus(core, dc, 2), plus(y, dy, NY)), device_id_type=MESH)
            greeted += 1
    for copy in loads:
        copy.wait()
    lanes = lax.broadcasted_iota(jnp.int32, (rank, ch), 1)
    tiled = jnp.concatenate([basis_ref[...]] * NY, axis=0).T
    placed = jnp.where(lax.div(lanes, CHG) == y, tiled, 0.0)
    bt[...] = placed.reshape(blocks, RB, ch)
    sampled = ks_ref[...] * mask_ref[...].astype(F32)
    own[...] = sampled
    edge[...] = jnp.where(core == 0, sampled[:, :PAD], sampled[:, HALF - PAD:])
    pl.semaphore_wait(barrier, greeted)

    waiting = []
    basis_in = []
    for dy, dc in peers:
        i = slot()
        yy, cc = plus(y, dy, NY), plus(core, dc, 2)
        waiting.append(start(bt.at[yy * 2 + cc], vx.at[core, y], dev(t, cc, yy), i))
        basis_in.append((plus(core, dc, 2), plus(y, NY - dy, NY), i))
    tile_in = []
    for dy, dc in peers:
        i = slot()
        yy, cc = plus(y, dy, NY), plus(core, dc, 2)
        waiting.append(start(own, sb.at[core, y], dev(t, cc, yy), i))
        tile_in.append((plus(core, dc, 2), plus(y, NY - dy, NY), i))
    halo_base = [slot() for _ in range(2 * NY)]
    target = lax.rem(t + tiles + 2 * core - 1, tiles)
    for dy, dc in ring:
        i = halo_base[dc * NY + dy]
        yy, cc = plus(y, dy, NY), plus(core, dc, 2)
        waiting.append(start(edge, halo.at[core, y], dev(target, cc, yy), i, halo_base[0] + core * NY + dy))
    vx[core, y] = bt[b]
    sb[core, y] = own[...]
    for cc, yy, i in basis_in:
        arrived(vx.at[cc, yy], i)
    halves = []
    for half in range(2):
        total = vx[half, 0]
        for yy in range(1, NY):
            total = total + vx[half, yy]
        halves.append(total)
    first_chunk = jnp.concatenate(halves, axis=1)

    pending = []

    def gather_start(it, chunk):
        vall[it, t] = chunk
        first = {}
        for k in near_first(NZ):
            first[k] = slot()
            pending.append(start(vall.at[it, t], vall.at[it, t], dev(at(plus(z, k, NZ), x), core, y), first[k]))
        second = []
        gather_relay((it, first, second), (0,))
        return it, first, second

    def gather_relay(state, steps):
        it, first, second = state
        for k in steps:
            zz = plus(z, NZ - k, NZ)
            here = at(zz, x)
            if k:
                arrived(vall.at[it, here], first[k])
            for q in range(1, NX):
                i = slot()
                pending.append(start(vall.at[it, here], vall.at[it, here], dev(at(z, plus(x, q, NX)), core, y), i))
                second.append((at(zz, plus(x, NX - q, NX)), i))

    def gather_finish(state, low=0, high=None):
        for here, i in state[2][low:high]:
            arrived(vall.at[state[0], here], i)

    def analyse(it):
        slabs = vall[it].reshape(NZ, NX, RB, 2 * ch)
        joined = jnp.concatenate(
            [slabs[:, q].reshape(NZ * RB, 2 * ch) for q in range(NX)], axis=1
        )
        high, low = split(joined)
        size = NZ * RB
        main = mm(jnp.concatenate([high, low], axis=0), s8h[...])
        product = main[:size] + main[size:] + mm(high, s8l[...])
        image = product[0:RB]
        for k in range(1, NZ):
            image = image + pltpu.roll(product[k * RB:(k + 1) * RB], width - 2 * NX * k, 1)
        return image

    def setup_tile():
        for cc, yy, i in tile_in:
            arrived(sb.at[cc, yy], i)
        for s in range(2):
            for dy in range(NY):
                arrived(halo.at[s, plus(y, NY - dy, NY)], halo_base[s * NY + dy])
        full = jnp.concatenate(
            [
                jnp.concatenate([halo[1, g], sb[0, g], sb[1, g], halo[0, g]], axis=1)
                for g in range(NY)
            ],
            axis=0,
        )
        for shift in range(2 * NX):
            moved = full if shift == 0 else pltpu.roll(full, width - shift, 1)
            high, low = split(moved)
            s8h[shift * ch:(shift + 1) * ch, :] = high
            s8l[shift * ch:(shift + 1) * ch, :] = low
        turned[0:width, :] = full.T
        turned[width:width + 8, :] = jnp.zeros((8, ch), F32)
        for shift in range(2 * NX):
            high, low = split(turned[shift:shift + width, :])
            s8th[:, shift * ch:(shift + 1) * ch] = high
            s8tl[:, shift * ch:(shift + 1) * ch] = low

    far_first = near_first(NZ)[::-1] + [0]

    def normal_start(it, image, hook=None):
        place = lax.broadcasted_iota(jnp.int32, (RB, width), 1)
        image = jnp.where(jnp.logical_and(place >= PAD, place < PAD + 2 * HALF), image, 0.0)
        moved = [image] + [pltpu.roll(image, 2 * NX * k, 1) for k in range(1, NZ)]
        high, low = split(jnp.concatenate(moved, axis=0))
        stacked = jnp.concatenate([high, low], axis=0)
        size = NZ * RB
        posts = {}
        for q in near_first(NX)[::-1] + [0]:
            if q == 0 and hook is not None:
                hook()
            xx = plus(x, q, NX)
            lanes_at = pl.ds(pl.multiple_of(xx * 2 * ch, 2 * ch), 2 * ch)
            main = mm(stacked, s8th[:, lanes_at])
            part = main[:size] + main[size:] + mm(high, s8tl[:, lanes_at])
            zp[it, xx] = part.reshape(NZ, RB, 2 * ch)
            for o, k in enumerate(far_first if q else ()):
                i = slot()
                pending.append(start(zp.at[it, xx, plus(z, k, NZ)], rx.at[it, q - 1, o], dev(at(z, xx), core, y), i))
                posts[q, o] = i
        return it, posts, [slot() for _ in range(NZ)]

    def normal_relay(state, o):
        it, posts, back = state
        zz = plus(z, far_first[o], NZ)
        for q in range(1, NX):
            arrived(rx.at[it, q - 1, o], posts[q, o])
        total = zp[it, x, zz]
        for q in range(1, NX):
            total = total + rx[it, q - 1, o]
        zs[it, o] = total
        if far_first[o]:
            i = back[far_first[o]]
            pending.append(start(zs.at[it, o], rz.at[it, z], dev(at(zz, x), core, y), i))

    def normal_finish(state):
        it, _, back = state
        mine = zs[it, NZ - 1]
        for k in range(1, NZ):
            source = plus(z, NZ - k, NZ)
            arrived(rz.at[it, source], back[k])
            mine = mine + rz[it, source]
        return mine

    def share(src, ref_of):
        posts = []
        for dy, dc in peers[::-1]:
            i = slot()
            yy, cc = plus(y, dy, NY), plus(core, dc, 2)
            pending.append(start(src, ref_of(b), dev(t, cc, yy), i))
            posts.append((plus(y, NY - dy, NY) * 2 + plus(core, dc, 2), i))
        return ref_of, posts

    def shared(state):
        ref_of, posts = state
        for bb, i in posts[::-1]:
            arrived(ref_of(bb), i)

    def rows_share(it, chunk):
        pz[it, b] = chunk
        return share(pz.at[it, b], lambda bb: pz.at[it, bb])

    def along_z(it, product):
        gz[it, z] = product
        posts = []
        for k in near_first(NZ)[::-1]:
            i = slot()
            pending.append(start(gz.at[it, z], gz.at[it, z], dev(at(plus(z, k, NZ), x), core, y), i))
            posts.append((plus(z, NZ - k, NZ), i))
        return it, posts

    def along_x(state):
        it, posts = state
        for zz, i in posts[::-1]:
            arrived(gz.at[it, zz], i)
        total = gz[it, 0]
        for k in range(1, NZ):
            total = total + gz[it, k]
        gx[it, x] = total
        posts = []
        for k in near_first(NX)[::-1]:
            i = slot()
            pending.append(start(gx.at[it, x], gx.at[it, x], dev(at(z, plus(x, k, NX)), core, y), i))
            posts.append((plus(x, NX - k, NX), i))
        return it, posts

    def gram_share(state):
        it, posts = state
        for xx, i in posts[::-1]:
            arrived(gx.at[it, xx], i)
        total = gx[it, 0]
        for k in range(1, NX):
            total = total + gx[it, k]
        gp[it, b] = total
        return share(gp.at[it, b], lambda bb: gp.at[it, bb])

    def factor_start(it):
        line = lax.broadcasted_iota(jnp.int32, (rank, rank), 0)
        column = lax.broadcasted_iota(jnp.int32, (rank, rank), 1)
        aug[:, :rank] = gp[it].reshape(rank, rank)
        aug[:, rank:] = jnp.where(line == column, 1.0, 0.0).astype(F32)

    def factor_panels(it, low, high):
        sub = lax.broadcasted_iota(jnp.int32, (PANEL, rank), 0)

        def panel(k, carry):
            top = pl.multiple_of(k * PANEL, PANEL)
            left = aug[pl.ds(top, PANEL), :rank]
            right = aug[pl.ds(top, PANEL), rank:]
            turned = pltpu.roll(left, lax.rem(rank - k * PANEL, rank), 1)
            cols = [jnp.broadcast_to(turned[:, q:q + 1], (PANEL, rank)) for q in range(PANEL)]
            done_left = jnp.zeros((PANEL, rank), F32)
            done_right = done_left

            def line(value, p):
                return jnp.broadcast_to(value[p:p + 1, :], (PANEL, rank))

            for p in range(PANEL):
                root = lax.rsqrt(line(cols[p], p))
                step = cols[p] * root
                for q in range(p + 1, PANEL):
                    cols[q] = cols[q] - step * (line(cols[q], p) * root)
                left_line = line(left, p) * root
                right_line = line(right, p) * root
                done_left = jnp.where(sub == p, left_line, done_left)
                done_right = jnp.where(sub == p, right_line, done_right)
                left = left - step * left_line
                right = right - step * right_line
            both = jnp.concatenate([done_left, done_right], axis=1)
            fac[it, pl.ds(top, PANEL), :] = done_right
            aug[...] = aug[...] - exact(done_left, both, ((0,), (0,)))
            return carry

        lax.fori_loop(low, high, panel, 0)

    panels = rank // PANEL
    order = near_first(NZ)
    moving = gather_start(0, first_chunk)
    gather_relay(moving, order)
    setup_tile()
    gather_finish(moving)
    folding = normal_start(0, analyse(0))
    for o in range(NZ):
        normal_relay(folding, o)
    chunk = normal_finish(folding)

    moving = gather_start(1, chunk)
    joined = rows_share(0, chunk)
    gather_relay(moving, order[:2])
    shared(joined)
    gram = along_z(0, exact(pz[0, b], pz[0].reshape(rank, 2 * ch), ((1,), (1,))))
    gather_relay(moving, order[2:])
    early = (NX - 1) * (NZ // 2)
    gather_finish(moving, 0, early)
    gram = along_x(gram)
    gather_finish(moving, early)
    grams = []
    folding = normal_start(1, analyse(1), lambda: grams.append(gram_share(gram)))
    gram = grams[0]
    head = max(NZ - 5, 1)
    for o in range(head):
        normal_relay(folding, o)
    shared(gram)
    factor_start(0)
    for o in range(head, NZ):
        factor_panels(0, o - head, o - head + 1)
        normal_relay(folding, o)
    factor_panels(0, NZ - head, panels)
    chunk = normal_finish(folding)
    joined = rows_share(1, chunk)
    shared(joined)
    vfull[...] = exact(fac[0], pz[1].reshape(rank, 2 * ch)).reshape(blocks, RB, 2 * ch)

    chunk = vfull[b]
    gram = along_z(1, exact(chunk, vfull[...].reshape(rank, 2 * ch), ((1,), (1,))))
    moving = gather_start(2 + core, chunk)
    gather_relay(moving, order[:4])
    gram = along_x(gram)
    gather_relay(moving, order[4:])
    gram = gram_share(gram)
    gather_finish(moving)
    other = 1 - core
    swap = slot()
    pending.append(start(vall.at[2 + core], vall.at[2 + core], dev(t, other, y), swap))
    image = analyse(2 + core)
    for half in range(2):
        ys[half] = image[:, half * HALF:half * HALF + span]
    yx[b] = ys[core]
    posts = []
    for dy, dc in peers[::-1]:
        i = slot()
        yy, cc = plus(y, dy, NY), plus(core, dc, 2)
        pending.append(start(ys.at[cc], yx.at[b], dev(t, cc, yy), i))
        posts.append((plus(y, NY - dy, NY) * 2 + plus(core, dc, 2), i))
    joined = (lambda bb: yx.at[bb]), posts
    arrived(vall.at[2 + other], swap)
    both_blocks = jnp.concatenate([vall[2], vall[3]], axis=1).reshape(tiles * 2 * RB, 2 * ch)
    turned_high, turned_low = split(both_blocks.T)
    shared(gram)
    factor_start(1)
    factor_panels(1, 0, panels)
    inverse = fac[1]
    fac[0] = inverse.T
    weights = exact(fac[0, pl.ds(pl.multiple_of(y * 2 * RB, 2 * RB), 2 * RB), :], inverse)
    shared(joined)
    high, low = split(weights)
    wide_high, wide_low = split(yx[...].reshape(rank, span))
    main = mm(jnp.concatenate([high, low], axis=0), wide_high)
    image = main[:2 * RB] + main[2 * RB:] + mm(high, wide_low)
    for i in range(tiles):
        high, low = split(image if i == 0 else pltpu.roll(image, 2 * i, 1))
        yh[i * 2 * RB:(i + 1) * 2 * RB, :] = high
        yl[i * 2 * RB:(i + 1) * 2 * RB, :] = low
    main = mm(jnp.concatenate([turned_high, turned_low], axis=0), yh[...])
    part = main[:2 * ch] + main[2 * ch:] + mm(turned_high, yl[...])
    total = part[:ch] + pltpu.roll(part[ch:], 1, 1)
    es[...] = total[:, PAD:].reshape(NY, CHG, HALF)
    back = []
    for dy in near_first(NY)[::-1]:
        j = slot()
        yy = plus(y, dy, NY)
        pending.append(start(es.at[yy], ey.at[dy], dev(t, core, yy), j))
        back.append((dy, j))
    estimate = es[y]
    both = exact(inverse, vfull[...].reshape(rank, 2 * ch))
    aug[:, :rank] = jnp.where(core == 0, both[:, :ch], both[:, ch:]).T
    bout_ref[...] = aug[pl.ds(pl.multiple_of(y * CHG, CHG), CHG), :rank]
    for copy in waiting + pending[:-(NY - 1)]:
        copy.wait_send()
    for dy, j in back:
        arrived(ey.at[dy], j)
        estimate = estimate + ey[dy]
    estimate = estimate * (1.0 / (2 * tiles))
    residual = mask_ref[...].astype(F32) * (ks_ref[...] - estimate)
    rec_ref[...] = estimate + residual - jnp.clip(residual, -THRESHOLD, THRESHOLD)
    for copy in pending[-(NY - 1):]:
        copy.wait_send()
    assert used[0] <= SEMS, used[0]


def shards(kspace, sample_mask, start_basis):
    tiles = NZ * NX
    ch = NY * CHG
    width = 2 * HALF + 2 * PAD
    span = HALF + PAD
    blocks = 2 * NY
    rank = blocks * RB
    vmem = pltpu.VMEM
    operands = (kspace, sample_mask, start_basis.reshape(CHG, rank))
    recovered, basis = pl.pallas_call(
        kernel,
        out_shape=(
            jax.ShapeDtypeStruct((CHG, HALF), F32),
            jax.ShapeDtypeStruct((CHG, rank), F32),
        ),
        in_specs=[pl.BlockSpec(memory_space=pltpu.HBM)] * 3,
        out_specs=(pl.BlockSpec(memory_space=pltpu.VMEM),) * 2,
        scratch_shapes=[
            vmem((CHG, HALF), F32),
            vmem((CHG, HALF), jnp.int32),
            vmem((CHG, rank), F32),
            vmem((CHG, HALF), F32),
            vmem((2, NY, CHG, HALF), F32),
            vmem((CHG, PAD), F32),
            vmem((2, NY, CHG, PAD), F32),
            vmem((blocks, RB, ch), F32),
            vmem((2, NY, RB, ch), F32),
            vmem((ITERS + 2, tiles, RB, 2 * ch), F32),
            vmem((2 * NX * ch, width), BF16),
            vmem((2 * NX * ch, width), BF16),
            vmem((width, 2 * NX * ch), BF16),
            vmem((width, 2 * NX * ch), BF16),
            vmem((width + 8, ch), F32),
            vmem((tiles * 2 * RB, span), BF16),
            vmem((tiles * 2 * RB, span), BF16),
            vmem((ITERS, NX, NZ, RB, 2 * ch), F32),
            vmem((ITERS, max(NX - 1, 1), NZ, RB, 2 * ch), F32),
            vmem((ITERS, NZ, RB, 2 * ch), F32),
            vmem((ITERS, NZ, RB, 2 * ch), F32),
            vmem((ITERS, blocks, RB, 2 * ch), F32),
            vmem((ITERS, NZ, RB, rank), F32),
            vmem((ITERS, NX, RB, rank), F32),
            vmem((ITERS, blocks, RB, rank), F32),
            vmem((rank, 2 * rank), F32),
            vmem((ITERS, rank, rank), F32),
            vmem((blocks, RB, 2 * ch), F32),
            vmem((2, RB, span), F32),
            vmem((blocks, RB, span), F32),
            vmem((NY, CHG, HALF), F32),
            vmem((NY, CHG, HALF), F32),
            pltpu.SemaphoreType.DMA((SEMS,)),
            pltpu.SemaphoreType.DMA((SEMS,)),
            pltpu.SemaphoreType.DMA((3,)),
        ],
        compiler_params=pltpu.CompilerParams(
            collective_id=0, has_side_effects=True, vmem_limit_bytes=48 << 20
        ),
    )(*[pltpu.with_memory_space_constraint(v, pltpu.HBM) for v in operands])
    return recovered, basis.reshape(1, CHG, rank)


def solution(mesh):
    return jax.shard_map(
        shards,
        mesh=mesh,
        in_specs=(P("coil", "rows"), P("coil", "rows"), P("coil", "rows", None)),
        out_specs=(P("coil", "rows"), P("coil", "rows", None)),
        check_vma=False,
    )
```
